128 devices in a mesh: leaf: 128 (over z, x, y, core).
Axes of the slice: x: 4, y: 4, z: 4, core: 2. Of those that a mesh axis runs over, the one named last changes fastest.
Arguments:
- points: bfloat16 [64, 524288], P(None, 'leaf'), may hold values from -3 to 7
- weights: bfloat16 [32, 524288], P(None, 'leaf'), may hold values from -6 to 6
- skel_index: int32 [65536], P('leaf'), may hold values from 0 to 4095, as said below
- assign: int32 [524288], P('leaf'), may hold values from 0 to 511
- near_leaf: int32 [1024, 12], replicated, may hold values from 0 to 1023, as said below
- near_count: int32 [1024], replicated, may hold values from 6 to 12
Outputs:
- near_field: float32 [32, 524288], P(None, 'leaf')
- far_field: float32 [32, 524288], P(None, 'leaf')
The draws below stay inside these ranges and needn't reach their ends.
Inputs may be any that keep to these rules, and one draw needn't show every extreme that they name: `skel_index`: each device's 512 entries are distinct. `near_leaf`: leaf id g belongs to device g // 8. For each device r, its 96 entries read leaf by leaf and taken in runs of 128 - 1 (the last run may be shorter) name leaves of devices other than r, of distinct devices within a run; so a device reads at most 1 block from any one device, and this is reached.
All inputs are finite; a program needn't handle non-finite values.
Results may differ from the reference program's by a relative error of at most 0.0088.
Values may be sent and summed in bfloat16 or wider, within the bound.
No kernel may reach another device: no remote copies, remote signals or barrier semaphores. Data moves between devices by JAX's collectives and lax.ppermute only.
A program may use at most 128 MiB of HBM per device.

```python
import math
import jax
import jax.numpy as jnp
from jax import lax

D = 64
RHS = 32
LEAF = 512
SKEL = 512
NEAR = 12
LEAVES_DEV = 8
LEAVES = 1024
POINTS = 524288
SKEL_ALL = 65536
LEVELS = 7
N_LEAF = 128


def draw_points(key, part):
    latent_key, noise_key = jax.random.split(jax.random.fold_in(key, 31))
    latent = jnp.clip(jax.random.normal(latent_key, (4, POINTS), jnp.float32), -3.5, 3.5)
    noise = jnp.clip(0.5 * jax.random.normal(noise_key, (D, POINTS), jnp.float32), -1.5, 1.5)
    centre = 2.0
    spread = jnp.tile(latent, (D // 4, 1))
    return (centre + spread + noise).astype(jnp.bfloat16)


def draw_skel_index(key, part):
    device_count = SKEL_ALL // SKEL
    p_dev = LEAVES_DEV * LEAF

    def one_device(dev_key):
        first_key, second_key = jax.random.split(dev_key)
        inner = 1 + jax.random.permutation(first_key, p_dev - 2)[:SKEL - 2]
        whole = jnp.concatenate([jnp.array([0, p_dev - 1], jnp.int32), inner.astype(jnp.int32)])
        return whole[jax.random.permutation(second_key, SKEL)]
    return jax.vmap(one_device)(jax.random.split(jax.random.fold_in(key, 5), device_count)).reshape(-1).astype(jnp.int32)


def draw_near_leaf(key, part):
    device_count = LEAVES // LEAVES_DEV
    slot_count = LEAVES_DEV * NEAR
    perm_key, local_key = jax.random.split(jax.random.fold_in(key, 11))

    def one_reader(reader_key, reader):
        offsets = (1 + jax.random.permutation(reader_key, device_count - 1)).astype(jnp.int32)
        spot = jnp.argmax((offsets == device_count - 1).astype(jnp.int32))
        forced = offsets.at[spot].set(offsets[0]).at[0].set(device_count - 1)
        offsets = jnp.where(reader < 2, forced, offsets)
        slot_pos = jnp.arange(slot_count, dtype=jnp.int32) % (device_count - 1)
        return (reader + offsets[slot_pos]) % device_count
    owners = jax.vmap(one_reader)(jax.random.split(perm_key, device_count), jnp.arange(device_count, dtype=jnp.int32))
    local_ids = jax.random.randint(local_key, (device_count, slot_count), 0, LEAVES_DEV).astype(jnp.int32)
    local_ids = local_ids.at[0, 0].set(LEAVES_DEV - 1).at[1, 0].set(0)
    return (owners * LEAVES_DEV + local_ids).reshape(LEAVES, NEAR).astype(jnp.int32)


def draw_near_count(key, part):
    device_count = LEAVES // LEAVES_DEV
    heavy_key, light_key = jax.random.split(jax.random.fold_in(key, 23))
    heavy = jax.random.randint(heavy_key, (device_count,), 0, 4) == 0
    heavy = heavy.at[0].set(True).at[1].set(False)
    light = jax.random.randint(light_key, (device_count, LEAVES_DEV), NEAR // 2, NEAR + 1).astype(jnp.int32)
    light = light.at[1, 0].set(NEAR // 2)
    counts = jnp.where(heavy[:, None], NEAR, light)
    return counts.reshape(LEAVES).astype(jnp.int32)


def plant(values, stream_key, least, high):
    extent = values.shape
    index_at = [jax.random.randint(jax.random.fold_in(stream_key, axis), (), 0, extent[axis]) for axis in range(len(extent))]
    values = values.at[tuple(index_at)].set(least)
    longest = extent.index(max(extent))
    index_at[longest] = (index_at[longest] + 1) % extent[longest]
    return values.at[tuple(index_at)].set(high)


def block_levels(stream_key, dims, cuts, low, largest):
    gain = 1.0
    for axis_at, blocks in cuts:
        heights = jax.random.uniform(jax.random.fold_in(jax.random.fold_in(stream_key, 6), axis_at), (blocks,), jnp.float32, low / len(cuts), largest / len(cuts))
        gain = gain * jnp.repeat(jnp.exp(heights), dims[axis_at] // blocks).reshape((-1,) + (1,) * (len(dims) - 1 - axis_at))
    return gain


def gaussian(rng, dims, scale, bound, shards=(), kind=jnp.bfloat16):
    drawn = jax.random.normal(rng, dims, jnp.float32) * scale
    if len(shards) > 0:
        drawn = block_levels(rng, dims, shards, -0.22, 0.18) * drawn
    return jnp.clip(drawn, min=-bound, max=bound).astype(kind)


def setup_inputs(seed: int = 0) -> dict:
    key_of = jax.random.split(jax.random.key(seed), 7)
    points = draw_points(jax.random.fold_in(key_of[6], 71), 0)
    weights = gaussian(key_of[1], (RHS, POINTS), 1.0, 6.0, ((1, 128),))
    skel_index = draw_skel_index(jax.random.fold_in(key_of[6], 71), 0)
    assign = plant(jax.random.randint(key_of[3], (POINTS,), 0, SKEL), jax.random.fold_in(key_of[3], 1), 0, SKEL - 1).astype(jnp.int32)
    near_leaf = draw_near_leaf(jax.random.fold_in(key_of[6], 71), 0)
    near_count = draw_near_count(jax.random.fold_in(key_of[6], 71), 0)
    return {"points": points, "weights": weights, "skel_index": skel_index, "assign": assign, "near_leaf": near_leaf, "near_count": near_count}


def kernel_apply(targets, sources, source_w):
    inner_prod = lax.dot_general(sources, targets, (((0,), (0,)), ((), ())), preferred_element_type=jnp.float32)
    target_sq = lax.optimization_barrier(jnp.sum(jnp.square(targets.astype(jnp.float32)), axis=0))
    source_sq = lax.optimization_barrier(jnp.sum(jnp.square(sources.astype(jnp.float32)), axis=0))
    sq_dist = source_sq[:, None] + target_sq[None, :] - 2.0 * inner_prod
    kernel_tile = jnp.exp(sq_dist * (-1.0 / D)).astype(jnp.bfloat16)
    return jnp.dot(source_w, kernel_tile, preferred_element_type=jnp.float32)

def fold_child(node_stack):
    half_width = node_stack.shape[-1] // 2
    node_weights = node_stack[..., D:, :half_width].astype(jnp.float32) + node_stack[..., D:, half_width:].astype(jnp.float32)
    return jnp.concatenate([node_stack[..., :D, :half_width], node_weights.astype(jnp.bfloat16)], axis=-2)

def merge_pair(lower_child, upper_child):
    return jnp.concatenate([fold_child(lower_child), fold_child(upper_child)], axis=-1)

def reference(points, weights, skel_index, assign, near_leaf, near_count):
    p_dev = LEAVES_DEV * LEAF
    stacked = jnp.concatenate([points, weights], axis=0)
    leaf_blocks = stacked.reshape(D + RHS, LEAVES, LEAF).transpose(1, 0, 2)

    def near_one(packed):
        leaf_ids, used, own_block = packed
        neighbours = leaf_blocks[leaf_ids]

        def one_term(source_block):
            return kernel_apply(own_block[:D], source_block[:D], source_block[D:])
        terms = jax.vmap(one_term)(neighbours)
        live_slot = (jnp.arange(NEAR, dtype=jnp.int32) < used).astype(jnp.float32)
        own_term = kernel_apply(own_block[:D], own_block[:D], own_block[D:])
        return own_term + lax.optimization_barrier(jnp.sum(terms * live_slot[:, None, None], axis=0))
    near_sum = lax.map(near_one, (near_leaf, near_count, leaf_blocks))
    near_field = near_sum.transpose(1, 0, 2).reshape(RHS, POINTS) * (4.0 / math.sqrt(LEAF * (NEAR + 1)))
    device_blocks = stacked.reshape(D + RHS, N_LEAF, p_dev).transpose(1, 0, 2)

    def base_one(packed):
        device_block, chosen, owner_skel = packed
        skel_points = device_block[:D][:, chosen]
        summed = jax.ops.segment_sum(device_block[D:].astype(jnp.float32).T, owner_skel, SKEL).T
        return jnp.concatenate([skel_points, summed.astype(jnp.bfloat16)], axis=0)
    node_stack = lax.map(base_one, (device_blocks, skel_index.reshape(N_LEAF, SKEL), assign.reshape(N_LEAF, p_dev)))
    device_ids = jnp.arange(N_LEAF, dtype=jnp.int32)
    far_sum = jnp.zeros((N_LEAF, RHS, p_dev), jnp.float32)

    def far_one(packed):
        device_block, partner = packed
        return kernel_apply(device_block[:D], partner[:D], partner[D:])
    for depth_bit in range(LEVELS):
        partners = node_stack[device_ids >> depth_bit ^ 1]
        far_sum = far_sum + lax.map(far_one, (device_blocks, partners))
        if depth_bit + 1 < LEVELS:
            node_stack = merge_pair(node_stack[0::2], node_stack[1::2])
    far_field = far_sum.transpose(1, 0, 2).reshape(RHS, POINTS) * (4.0 / math.sqrt(POINTS))
    return (near_field, far_field)
```

```python
import functools
import math

import jax
import jax.numpy as jnp
from jax import lax
from jax.experimental import pallas as pl
from jax.experimental.pallas import tpu as pltpu
from jax.sharding import Mesh, PartitionSpec as P

D = 64
RHS = 32
LEAF = 512
SKEL = 512
NEAR = 12
LEAVES_DEV = 8
P_DEV = LEAF * LEAVES_DEV
ROWS = D + RHS
N_DEV = 128
SIZES = {"z": 4, "x": 4, "y": 4, "core": 2}
AXES = ("z", "x", "y", "core")
DEPTH = 2 * D + 16
UNROLL = 4
SLOTS = LEAVES_DEV * NEAR
LOG = math.log2(math.e) / D
NEAR_SCALE = 4.0 / math.sqrt(LEAF * (NEAR + 1))
FAR_SCALE = 4.0 / math.sqrt(P_DEV * N_DEV)
LINE = (2, 1, 3, 0)


def shift(block, axis, by):
    count = SIZES[axis]
    return lax.ppermute(block, axis, [(i, (i + by) % count) for i in range(count)])


def swap(block, axis, bit):
    count = SIZES[axis]
    return lax.ppermute(block, axis, [(i, i ^ bit) for i in range(count)])


def norm_rows(coords, first):
    width = coords.shape[1]
    rest = jnp.sum(coords * coords, axis=0, keepdims=True) * (-LOG)
    row = lax.broadcasted_iota(jnp.int32, (16, width), 0)
    rows = jnp.where(row < 6, 1.0, 0.0)
    for part in range(3):
        piece = rest.astype(jnp.bfloat16).astype(jnp.float32)
        rest = rest - piece
        rows = jnp.where(row == first + part, piece, rows)
    return rows.astype(jnp.bfloat16)


def put_source(aug, coords):
    aug[0:D, :] = coords
    aug[D : 2 * D, :] = coords
    aug[2 * D :, :] = norm_rows(coords.astype(jnp.float32), 0)


def put_target(aug, coords):
    wide = coords.astype(jnp.float32)
    scaled = wide * (2.0 * LOG)
    high = scaled.astype(jnp.bfloat16)
    aug[0:D, :] = high
    aug[D : 2 * D, :] = (scaled - high.astype(jnp.float32)).astype(jnp.bfloat16)
    aug[2 * D :, :] = norm_rows(wide, 3)


def tile_apply(source_aug, target_aug, source_w):
    power = lax.dot_general(
        source_aug, target_aug, (((0,), (0,)), ((), ())), preferred_element_type=jnp.float32
    )
    tile = jnp.exp2(power).astype(jnp.bfloat16)
    return jnp.dot(source_w, tile, preferred_element_type=jnp.float32)


def own_kernel(block_ref, node_ref, self_ref, far_ref, target_aug, source_aug):
    for leaf in range(LEAVES_DEV):
        cols = slice(leaf * LEAF, (leaf + 1) * LEAF)
        put_target(target_aug.at[:, cols], block_ref[0:D, cols])

    @pl.loop(0, LEAVES_DEV // UNROLL)
    def _(group):
        for unit in range(UNROLL):
            start = pl.multiple_of((group * UNROLL + unit) * LEAF, LEAF)
            cols = pl.ds(start, LEAF)
            put_source(source_aug.at[unit], block_ref[0:D, cols])
            self_ref[:, cols] = tile_apply(
                source_aug[unit], target_aug[:, cols], block_ref[D:ROWS, cols]
            )

    far_ref[...] = jnp.zeros_like(far_ref)

    @pl.loop(0, node_ref.shape[0])
    def _(level):
        put_source(source_aug.at[0], node_ref[level, 0:D])
        far_ref[...] += tile_apply(source_aug[0], target_aug[...], node_ref[level, D:ROWS])

    far_ref[...] = far_ref[...] * FAR_SCALE


def own_terms(own_block, nodes):
    shape = jax.ShapeDtypeStruct((RHS, P_DEV), jnp.float32)
    levels = nodes.shape[0]
    entries = (levels * SKEL + LEAF) * P_DEV
    return pl.pallas_call(
        own_kernel,
        out_shape=(shape, shape),
        in_specs=[pl.BlockSpec(memory_space=pltpu.VMEM)] * 2,
        out_specs=(pl.BlockSpec(memory_space=pltpu.VMEM),) * 2,
        scratch_shapes=[
            pltpu.VMEM((DEPTH, P_DEV), jnp.bfloat16),
            pltpu.VMEM((UNROLL, DEPTH, LEAF), jnp.bfloat16),
        ],
        compiler_params=pltpu.CompilerParams(vmem_limit_bytes=40 << 20),
        cost_estimate=pl.CostEstimate(
            flops=entries * 2 * (DEPTH + RHS), transcendentals=entries, bytes_accessed=3 << 20
        ),
    )(own_block, nodes)


def near_kernel(scale, pair_ref, count_ref, target_ref, source_ref, out_ref, buf, sem, target_aug, source_aug, acc):
    groups = (count_ref[0] + (UNROLL - 1)) // UNROLL

    def copy(group, slot, unit):
        code = pair_ref[group * UNROLL + unit]
        block = code % 256
        col = pl.multiple_of((block % LEAVES_DEV) * LEAF, LEAF)
        return pltpu.make_async_copy(
            source_ref.at[block // LEAVES_DEV, :, pl.ds(col, LEAF)],
            buf.at[slot, unit],
            sem.at[slot, unit],
        )

    @pl.when(groups > 0)
    def _():
        for unit in range(UNROLL):
            copy(0, 0, unit).start()

    for leaf in range(LEAVES_DEV):
        put_target(target_aug.at[leaf], target_ref[0:D, leaf * LEAF : (leaf + 1) * LEAF])
    acc[...] = jnp.zeros_like(acc)

    @pl.loop(0, groups)
    def _(group):
        slot = group % 2

        @pl.when(group + 1 < groups)
        def _():
            for unit in range(UNROLL):
                copy(group + 1, 1 - slot, unit).start()

        for unit in range(UNROLL):
            copy(group, slot, unit).wait()
        for unit in range(UNROLL):
            target = pair_ref[group * UNROLL + unit] // 256
            put_source(source_aug.at[unit], buf[slot, unit, 0:D])
            acc[target] += tile_apply(
                source_aug[unit],
                target_aug[jnp.minimum(target, LEAVES_DEV - 1)],
                buf[slot, unit, D:ROWS],
            )

    for leaf in range(LEAVES_DEV):
        out_ref[:, leaf * LEAF : (leaf + 1) * LEAF] = acc[leaf].astype(out_ref.dtype)


def near_part(pairs, count, target, sources, dtype):
    entries = 24 * LEAF * LEAF
    return pl.pallas_call(
        functools.partial(near_kernel, 1.0),
        out_shape=jax.ShapeDtypeStruct((RHS, P_DEV), dtype),
        in_specs=[
            pl.BlockSpec(memory_space=pltpu.SMEM),
            pl.BlockSpec(memory_space=pltpu.SMEM),
            pl.BlockSpec(memory_space=pltpu.VMEM),
            pl.BlockSpec(memory_space=pl.ANY),
        ],
        out_specs=pl.BlockSpec(memory_space=pltpu.VMEM),
        scratch_shapes=[
            pltpu.VMEM((2, UNROLL, ROWS, LEAF), jnp.bfloat16),
            pltpu.SemaphoreType.DMA((2, UNROLL)),
            pltpu.VMEM((LEAVES_DEV, DEPTH, LEAF), jnp.bfloat16),
            pltpu.VMEM((UNROLL, DEPTH, LEAF), jnp.bfloat16),
            pltpu.VMEM((LEAVES_DEV + 1, RHS, LEAF), jnp.float32),
        ],
        compiler_params=pltpu.CompilerParams(vmem_limit_bytes=40 << 20),
        cost_estimate=pl.CostEstimate(
            flops=entries * 2 * (DEPTH + RHS), transcendentals=entries, bytes_accessed=4 << 20
        ),
    )(pairs, count, target, sources)


def fold(weights):
    half = weights.shape[-1] // 2
    summed = weights[:, :half].astype(jnp.float32) + weights[:, half:].astype(jnp.float32)
    return summed.astype(jnp.bfloat16)


def fold_node(node):
    half = SKEL // 2
    return jnp.concatenate([node[:D, :half], fold(node[D:])], axis=0)


def sibling_nodes(base, place):
    found = []
    current = base
    steps = [("core", 1)] + [(axis, bit) for axis in ("y", "x", "z") for bit in (1, 2)]
    for level, (axis, bit) in enumerate(steps):
        partner = swap(current, axis, bit)
        found.append(partner)
        if level + 1 < len(steps):
            upper = (place[axis] // bit) % 2
            mine, theirs = fold_node(current), fold_node(partner)
            current = jnp.concatenate(
                [jnp.where(upper == 0, mine, theirs), jnp.where(upper == 0, theirs, mine)], axis=1
            )
    return jnp.stack(found)


def pair_lists(near_leaf, near_count, place):
    rows, counts = [], []
    for by in LINE:
        y = (place["y"] + by) % SIZES["y"]
        device = ((place["z"] * 4 + place["x"]) * 4 + y) * 2 + place["core"]
        rows.append(lax.dynamic_slice_in_dim(near_leaf, device * LEAVES_DEV, LEAVES_DEV))
        counts.append(lax.dynamic_slice_in_dim(near_count, device * LEAVES_DEV, LEAVES_DEV))
    leaf_ids = jnp.stack(rows)
    used = jnp.arange(NEAR, dtype=jnp.int32)[None, None, :] < jnp.stack(counts)[:, :, None]
    owner = leaf_ids // LEAVES_DEV
    here = (owner // 2) % 4 == place["y"]
    valid = (used & here).reshape(len(LINE), SLOTS)
    gathered = (owner // 8) * 2 + owner % 2
    target = jnp.arange(LEAVES_DEV, dtype=jnp.int32)[None, :, None]
    code = (target * 256 + gathered * LEAVES_DEV + leaf_ids % LEAVES_DEV).reshape(len(LINE), SLOTS)
    slot = jnp.arange(SLOTS, dtype=jnp.int32)
    before = jnp.sum(
        (valid[:, None, :] & (slot[None, None, :] < slot[None, :, None])).astype(jnp.int32), axis=2
    )
    total = jnp.sum(valid.astype(jnp.int32), axis=1)
    hit = valid[:, None, :] & (before[:, None, :] == slot[None, :, None])
    packed = jnp.sum(jnp.where(hit, code[:, None, :], 0), axis=2)
    spare = LEAVES_DEV * 256
    return jnp.where(slot[None, :] < total[:, None], packed, spare), total


def per_device(points, weights, skel_index, assign, near_leaf, near_count):
    place = {axis: lax.axis_index(axis) for axis in AXES}
    own_block = jnp.concatenate([points, weights], axis=0)
    sources = lax.all_gather(own_block, ("z", "x", "core"))
    targets = [shift(points, "y", -by) if by else points for by in LINE]

    member = (assign[None, :] == jnp.arange(SKEL, dtype=jnp.int32)[:, None]).astype(jnp.bfloat16)
    base_weights = lax.dot_general(
        weights, member, (((1,), (1,)), ((), ())), preferred_element_type=jnp.float32
    )
    base = jnp.concatenate([points[:, skel_index], base_weights.astype(jnp.bfloat16)], axis=0)
    nodes = sibling_nodes(base, place)
    self_sum, far_field = own_terms(own_block, nodes)

    pairs, total = pair_lists(near_leaf, near_count, place)
    near_sum = self_sum
    for at, by in enumerate(LINE):
        part = near_part(
            pairs[at], total[at : at + 1], targets[at], sources, jnp.bfloat16 if by else jnp.float32
        )
        near_sum = near_sum + (shift(part, "y", by) if by else part).astype(jnp.float32)
    return (near_sum * NEAR_SCALE, far_field)


def solution(mesh):
    grid = Mesh(mesh.devices.reshape([SIZES[axis] for axis in AXES]), AXES)
    split = P(None, AXES)
    return jax.shard_map(
        per_device,
        mesh=grid,
        in_specs=(split, split, P(AXES), P(AXES), P(), P()),
        out_specs=(split, split),
        check_vma=False,
    )
```

```python
import functools
import math

import jax
import jax.numpy as jnp
from jax import lax
from jax.experimental import pallas as pl
from jax.experimental.pallas import tpu as pltpu
from jax.sharding import Mesh, PartitionSpec as P

D = 64
RHS = 32
LEAF = 512
SKEL = 512
NEAR = 12
LEAVES_DEV = 8
P_DEV = LEAF * LEAVES_DEV
ROWS = D + RHS
N_DEV = 128
SIZES = {"z": 4, "x": 4, "y": 4, "core": 2}
AXES = ("z", "x", "y", "core")
DEPTH = 2 * D + 16
UNROLL = 4
SLOTS = LEAVES_DEV * NEAR
LOG = math.log2(math.e) / D
NEAR_SCALE = 4.0 / math.sqrt(LEAF * (NEAR + 1))
FAR_SCALE = 4.0 / math.sqrt(P_DEV * N_DEV)
LINE = (2, 1, 3, 0)


def shift(block, axis, by):
    count = SIZES[axis]
    return lax.ppermute(block, axis, [(i, (i + by) % count) for i in range(count)])


def swap(block, axis, bit):
    count = SIZES[axis]
    return lax.ppermute(block, axis, [(i, i ^ bit) for i in range(count)])


def norm_rows(coords, first):
    width = coords.shape[1]
    rest = jnp.sum(coords * coords, axis=0, keepdims=True) * (-LOG)
    row = lax.broadcasted_iota(jnp.int32, (16, width), 0)
    rows = jnp.where(row < 6, 1.0, 0.0)
    for part in range(3):
        piece = rest.astype(jnp.bfloat16).astype(jnp.float32)
        rest = rest - piece
        rows = jnp.where(row == first + part, piece, rows)
    return rows.astype(jnp.bfloat16)


def put_source(aug, coords):
    aug[0:D, :] = coords
    aug[D : 2 * D, :] = coords
    aug[2 * D :, :] = norm_rows(coords.astype(jnp.float32), 0)


def put_target(aug, coords):
    wide = coords.astype(jnp.float32)
    scaled = wide * (2.0 * LOG)
    high = scaled.astype(jnp.bfloat16)
    aug[0:D, :] = high
    aug[D : 2 * D, :] = (scaled - high.astype(jnp.float32)).astype(jnp.bfloat16)
    aug[2 * D :, :] = norm_rows(wide, 3)


def tile_apply(source_aug, target_aug, source_w):
    power = lax.dot_general(
        source_aug, target_aug, (((0,), (0,)), ((), ())), preferred_element_type=jnp.float32
    )
    tile = jnp.exp2(power).astype(jnp.bfloat16)
    return jnp.dot(source_w, tile, preferred_element_type=jnp.float32)


def own_kernel(block_ref, node_ref, self_ref, far_ref, target_aug, source_aug):
    for leaf in range(LEAVES_DEV):
        cols = slice(leaf * LEAF, (leaf + 1) * LEAF)
        put_target(target_aug.at[:, cols], block_ref[0:D, cols])

    @pl.loop(0, LEAVES_DEV // UNROLL)
    def _(group):
        for unit in range(UNROLL):
            start = pl.multiple_of((group * UNROLL + unit) * LEAF, LEAF)
            cols = pl.ds(start, LEAF)
            put_source(source_aug.at[unit], block_ref[0:D, cols])
            self_ref[:, cols] = tile_apply(
                source_aug[unit], target_aug[:, cols], block_ref[D:ROWS, cols]
            )

    far_ref[...] = jnp.zeros_like(far_ref)

    @pl.loop(0, node_ref.shape[0])
    def _(level):
        put_source(source_aug.at[0], node_ref[level, 0:D])
        far_ref[...] += tile_apply(source_aug[0], target_aug[...], node_ref[level, D:ROWS])

    far_ref[...] = far_ref[...] * FAR_SCALE


def own_terms(own_block, nodes):
    shape = jax.ShapeDtypeStruct((RHS, P_DEV), jnp.float32)
    levels = nodes.shape[0]
    entries = (levels * SKEL + LEAF) * P_DEV
    return pl.pallas_call(
        own_kernel,
        out_shape=(shape, shape),
        in_specs=[pl.BlockSpec(memory_space=pltpu.VMEM)] * 2,
        out_specs=(pl.BlockSpec(memory_space=pltpu.VMEM),) * 2,
        scratch_shapes=[
            pltpu.VMEM((DEPTH, P_DEV), jnp.bfloat16),
            pltpu.VMEM((UNROLL, DEPTH, LEAF), jnp.bfloat16),
        ],
        compiler_params=pltpu.CompilerParams(vmem_limit_bytes=40 << 20),
        cost_estimate=pl.CostEstimate(
            flops=entries * 2 * (DEPTH + RHS), transcendentals=entries, bytes_accessed=3 << 20
        ),
    )(own_block, nodes)


def near_kernel(scale, pair_ref, count_ref, target_ref, source_ref, out_ref, buf, sem, target_aug, source_aug, acc):
    groups = (count_ref[0] + (UNROLL - 1)) // UNROLL

    def copy(group, slot, unit):
        code = pair_ref[group * UNROLL + unit]
        block = code % 256
        col = pl.multiple_of((block % LEAVES_DEV) * LEAF, LEAF)
        return pltpu.make_async_copy(
            source_ref.at[block // LEAVES_DEV, :, pl.ds(col, LEAF)],
            buf.at[slot, unit],
            sem.at[slot, unit],
        )

    @pl.when(groups > 0)
    def _():
        for unit in range(UNROLL):
            copy(0, 0, unit).start()

    for leaf in range(LEAVES_DEV):
        put_target(target_aug.at[leaf], target_ref[0:D, leaf * LEAF : (leaf + 1) * LEAF])
    acc[...] = jnp.zeros_like(acc)

    @pl.loop(0, groups)
    def _(group):
        slot = group % 2

        @pl.when(group + 1 < groups)
        def _():
            for unit in range(UNROLL):
                copy(group + 1, 1 - slot, unit).start()

        for unit in range(UNROLL):
            copy(group, slot, unit).wait()
        for unit in range(UNROLL):
            target = pair_ref[group * UNROLL + unit] // 256
            put_source(source_aug.at[unit], buf[slot, unit, 0:D])
            acc[target] += tile_apply(
                source_aug[unit],
                target_aug[jnp.minimum(target, LEAVES_DEV - 1)],
                buf[slot, unit, D:ROWS],
            )

    for leaf in range(LEAVES_DEV):
        out_ref[:, leaf * LEAF : (leaf + 1) * LEAF] = acc[leaf].astype(out_ref.dtype)


def near_part(pairs, count, target, sources, dtype):
    entries = 24 * LEAF * LEAF
    return pl.pallas_call(
        functools.partial(near_kernel, 1.0),
        out_shape=jax.ShapeDtypeStruct((RHS, P_DEV), dtype),
        in_specs=[
            pl.BlockSpec(memory_space=pltpu.SMEM),
            pl.BlockSpec(memory_space=pltpu.SMEM),
            pl.BlockSpec(memory_space=pltpu.VMEM),
            pl.BlockSpec(memory_space=pl.ANY),
        ],
        out_specs=pl.BlockSpec(memory_space=pltpu.VMEM),
        scratch_shapes=[
            pltpu.VMEM((2, UNROLL, ROWS, LEAF), jnp.bfloat16),
            pltpu.SemaphoreType.DMA((2, UNROLL)),
            pltpu.VMEM((LEAVES_DEV, DEPTH, LEAF), jnp.bfloat16),
            pltpu.VMEM((UNROLL, DEPTH, LEAF), jnp.bfloat16),
            pltpu.VMEM((LEAVES_DEV + 1, RHS, LEAF), jnp.float32),
        ],
        compiler_params=pltpu.CompilerParams(vmem_limit_bytes=40 << 20),
        cost_estimate=pl.CostEstimate(
            flops=entries * 2 * (DEPTH + RHS), transcendentals=entries, bytes_accessed=4 << 20
        ),
    )(pairs, count, target, sources)


def fold(weights):
    half = weights.shape[-1] // 2
    summed = weights[:, :half].astype(jnp.float32) + weights[:, half:].astype(jnp.float32)
    return summed.astype(jnp.bfloat16)


def fold_node(node):
    half = SKEL // 2
    return jnp.concatenate([node[:D, :half], fold(node[D:])], axis=0)


def sibling_nodes(base, place):
    found = []
    current = base
    steps = [("core", 1)] + [(axis, bit) for axis in ("y", "x", "z") for bit in (1, 2)]
    for level, (axis, bit) in enumerate(steps):
        partner = swap(current, axis, bit)
        found.append(partner)
        if level + 1 < len(steps):
            upper = (place[axis] // bit) % 2
            mine, theirs = fold_node(current), fold_node(partner)
            current = jnp.concatenate(
                [jnp.where(upper == 0, mine, theirs), jnp.where(upper == 0, theirs, mine)], axis=1
            )
    return jnp.stack(found)


def pair_lists(near_leaf, near_count, place):
    rows, counts = [], []
    for by in LINE:
        y = (place["y"] + by) % SIZES["y"]
        device = ((place["z"] * 4 + place["x"]) * 4 + y) * 2 + place["core"]
        rows.append(lax.dynamic_slice_in_dim(near_leaf, device * LEAVES_DEV, LEAVES_DEV))
        counts.append(lax.dynamic_slice_in_dim(near_count, device * LEAVES_DEV, LEAVES_DEV))
    leaf_ids = jnp.stack(rows)
    used = jnp.arange(NEAR, dtype=jnp.int32)[None, None, :] < jnp.stack(counts)[:, :, None]
    owner = leaf_ids // LEAVES_DEV
    here = (owner // 2) % 4 == place["y"]
    valid = (used & here).reshape(len(LINE), SLOTS)
    gathered = (owner // 8) * 2 + owner % 2
    target = jnp.arange(LEAVES_DEV, dtype=jnp.int32)[None, :, None]
    code = (target * 256 + gathered * LEAVES_DEV + leaf_ids % LEAVES_DEV).reshape(len(LINE), SLOTS)
    slot = jnp.arange(SLOTS, dtype=jnp.int32)
    before = jnp.sum(
        (valid[:, None, :] & (slot[None, None, :] < slot[None, :, None])).astype(jnp.int32), axis=2
    )
    total = jnp.sum(valid.astype(jnp.int32), axis=1)
    hit = valid[:, None, :] & (before[:, None, :] == slot[None, :, None])
    packed = jnp.sum(jnp.where(hit, code[:, None, :], 0), axis=2)
    spare = LEAVES_DEV * 256
    return jnp.where(slot[None, :] < total[:, None], packed, spare), total


def per_device(points, weights, skel_index, assign, near_leaf, near_count):
    place = {axis: lax.axis_index(axis) for axis in AXES}
    own_block = jnp.concatenate([points, weights], axis=0)
    sources = lax.all_gather(own_block, ("z", "x", "core"))
    targets = [shift(points, "y", -by) if by else points for by in LINE]

    member = (assign[None, :] == jnp.arange(SKEL, dtype=jnp.int32)[:, None]).astype(jnp.bfloat16)
    base_weights = lax.dot_general(
        weights, member, (((1,), (1,)), ((), ())), preferred_element_type=jnp.float32
    )
    base = jnp.concatenate([points[:, skel_index], base_weights.astype(jnp.bfloat16)], axis=0)
    nodes = sibling_nodes(base, place)
    self_sum, far_field = own_terms(own_block, nodes)
    sources, self_sum, far_field = lax.optimization_barrier((sources, self_sum, far_field))

    pairs, total = pair_lists(near_leaf, near_count, place)
    near_sum = self_sum
    for at, by in enumerate(LINE):
        part = near_part(
            pairs[at], total[at : at + 1], targets[at], sources, jnp.bfloat16 if by else jnp.float32
        )
        near_sum = near_sum + (shift(part, "y", by) if by else part).astype(jnp.float32)
    return (near_sum * NEAR_SCALE, far_field)


def solution(mesh):
    grid = Mesh(mesh.devices.reshape([SIZES[axis] for axis in AXES]), AXES)
    split = P(None, AXES)
    return jax.shard_map(
        per_device,
        mesh=grid,
        in_specs=(split, split, P(AXES), P(AXES), P(), P()),
        out_specs=(split, split),
        check_vma=False,
    )
```

```python
import functools
import math

import jax
import jax.numpy as jnp
from jax import lax
from jax.experimental import pallas as pl
from jax.experimental.pallas import tpu as pltpu
from jax.sharding import Mesh, PartitionSpec as P

D = 64
RHS = 32
LEAF = 512
SKEL = 512
NEAR = 12
LEAVES_DEV = 8
P_DEV = LEAF * LEAVES_DEV
ROWS = D + RHS
N_DEV = 128
SIZES = {"z": 4, "x": 4, "y": 4, "core": 2}
AXES = ("z", "x", "y", "core")
DEPTH = D + 16
UNROLL = 4
GAIN = 2.0 * math.log2(math.e) / D
NEAR_SCALE = 4.0 / math.sqrt(LEAF * (NEAR + 1))
FAR_SCALE = 4.0 / math.sqrt(P_DEV * N_DEV)
LINE = (2, 1, 3, 0)
CLASS = LEAVES_DEV // 2
LISTS = (192, 32, 24, 8)
STARTS = (0, 192, 224, 248)
SPARE = 2 * len(LINE) * LEAVES_DEV


def shift(block, axis, by):
    count = SIZES[axis]
    return lax.ppermute(block, axis, [(i, (i + by) % count) for i in range(count)])


def swap(block, axis, bit):
    count = SIZES[axis]
    return lax.ppermute(block, axis, [(i, i ^ bit) for i in range(count)])


def ring(block, by, stage):
    route = []
    for flat in range(N_DEV):
        z, x, y, core = flat // 32, flat // 8 % 4, flat // 2 % 4, flat % 2
        if core == stage:
            z = (z + by) % 4
        else:
            x = (x + by) % 4
        route.append((flat, ((z * 4 + x) * 4 + y) * 2 + core))
    return lax.ppermute(block, AXES, route)


def put_points(aug, coords, first):
    width = coords.shape[1]
    aug[0:D, :] = coords
    wide = coords.astype(jnp.float32)
    rest = jnp.sum(wide * wide, axis=0, keepdims=True) * -0.5
    row = lax.broadcasted_iota(jnp.int32, (16, width), 0)
    rows = jnp.where(row < 6, 1.0, 0.0)
    for part in range(3):
        piece = rest.astype(jnp.bfloat16).astype(jnp.float32)
        rest = rest - piece
        rows = jnp.where(row == first + part, piece, rows)
    aug[D:, :] = rows.astype(jnp.bfloat16)


def tile_apply(source_aug, target_aug, source_w):
    power = lax.dot_general(
        source_aug, target_aug, (((0,), (0,)), ((), ())), preferred_element_type=jnp.float32
    )
    tile = jnp.exp2(power * GAIN).astype(jnp.bfloat16)
    return jnp.dot(source_w, tile, preferred_element_type=jnp.float32)


def cost(entries, moved):
    return pl.CostEstimate(
        flops=int(entries) * 2 * (DEPTH + RHS), transcendentals=int(entries), bytes_accessed=moved
    )


VMEM = pl.BlockSpec(memory_space=pltpu.VMEM)
SMEM = pl.BlockSpec(memory_space=pltpu.SMEM)
ANY = pl.BlockSpec(memory_space=pl.ANY)


def self_kernel(points_ref, weights_ref, out_ref, target_aug, source_aug):
    @pl.loop(0, LEAVES_DEV // UNROLL)
    def _(group):
        for unit in range(UNROLL):
            start = pl.multiple_of((group * UNROLL + unit) * LEAF, LEAF)
            cols = pl.ds(start, LEAF)
            put_points(source_aug.at[unit], points_ref[:, cols], 0)
            put_points(target_aug.at[unit], points_ref[:, cols], 3)
            out_ref[:, cols] = tile_apply(source_aug[unit], target_aug[unit], weights_ref[:, cols])


def self_terms(points, weights):
    return pl.pallas_call(
        self_kernel,
        out_shape=jax.ShapeDtypeStruct((RHS, P_DEV), jnp.float32),
        in_specs=[VMEM, VMEM],
        out_specs=VMEM,
        scratch_shapes=[pltpu.VMEM((UNROLL, DEPTH, LEAF), jnp.bfloat16)] * 2,
        compiler_params=pltpu.CompilerParams(vmem_limit_bytes=24 << 20),
        cost_estimate=cost(LEAF * P_DEV, 2 << 20),
    )(points, weights)


def far_kernel(points_ref, node_ref, far_ref, target_aug, source_aug):
    for leaf in range(LEAVES_DEV):
        cols = slice(leaf * LEAF, (leaf + 1) * LEAF)
        put_points(target_aug.at[:, cols], points_ref[:, cols], 3)
    far_ref[...] = jnp.zeros_like(far_ref)

    @pl.loop(0, node_ref.shape[0])
    def _(level):
        put_points(source_aug, node_ref[level, 0:D], 0)
        far_ref[...] += tile_apply(source_aug[...], target_aug[...], node_ref[level, D:ROWS])

    far_ref[...] = far_ref[...] * FAR_SCALE


def far_terms(points, nodes):
    levels = nodes.shape[0]
    return pl.pallas_call(
        far_kernel,
        out_shape=jax.ShapeDtypeStruct((RHS, P_DEV), jnp.float32),
        in_specs=[VMEM, VMEM],
        out_specs=VMEM,
        scratch_shapes=[
            pltpu.VMEM((DEPTH, P_DEV), jnp.bfloat16),
            pltpu.VMEM((DEPTH, SKEL), jnp.bfloat16),
        ],
        compiler_params=pltpu.CompilerParams(vmem_limit_bytes=24 << 20),
        cost_estimate=cost(levels * SKEL * P_DEV, 2 << 20),
    )(points, nodes)


def near_kernel(first, devices, n_source, seeded, pair_ref, count_ref, target_ref, *refs):
    source_refs, refs = refs[:n_source], refs[n_source:]
    if seeded:
        seed_ref, refs = refs[0], refs[1:]
    out_ref, buf, target_buf, sem, target_aug, source_aug, acc = refs
    leaves = devices * LEAVES_DEV
    groups = (count_ref[0] + (UNROLL - 1)) // UNROLL

    def fetch(group, slot):
        for unit in range(UNROLL):
            code = pair_ref[group * UNROLL + unit]
            target = jnp.minimum(code // (32 * CLASS), SPARE - 1)
            start = pl.multiple_of(target % LEAVES_DEV * LEAF, LEAF)
            pltpu.make_async_copy(
                target_ref.at[target // LEAVES_DEV, :, pl.ds(start, LEAF)],
                target_buf.at[slot, unit],
                sem.at[slot, unit, 1],
            ).start()
            which = code // (4 * CLASS) % 8
            start = pl.multiple_of(code % CLASS * LEAF, LEAF)
            for at in range(n_source):

                @pl.when(which == at)
                def _():
                    pltpu.make_async_copy(
                        source_refs[at].at[code // CLASS % 4, :, pl.ds(start, LEAF)],
                        buf.at[slot, unit],
                        sem.at[slot, unit, 0],
                    ).start()

    def arrive(slot):
        for unit in range(UNROLL):
            pltpu.make_async_copy(
                source_refs[0].at[0, :, pl.ds(0, LEAF)], buf.at[slot, unit], sem.at[slot, unit, 0]
            ).wait()
            pltpu.make_async_copy(
                target_ref.at[0, :, pl.ds(0, LEAF)], target_buf.at[slot, unit], sem.at[slot, unit, 1]
            ).wait()

    @pl.when(groups > 0)
    def _():
        fetch(0, 0)

    if seeded:
        for leaf in range(leaves):
            start = leaf % LEAVES_DEV * LEAF
            acc[leaf] = seed_ref[leaf // LEAVES_DEV, :, start : start + LEAF]
    else:
        acc[...] = jnp.zeros_like(acc)

    @pl.loop(0, groups)
    def _(group):
        slot = group % 2

        @pl.when(group + 1 < groups)
        def _():
            fetch(group + 1, 1 - slot)

        arrive(slot)
        for unit in range(UNROLL):
            target = pair_ref[group * UNROLL + unit] // (32 * CLASS)
            put_points(source_aug.at[unit], buf[slot, unit, 0:D], 0)
            put_points(target_aug.at[unit], target_buf[slot, unit], 3)
            acc[jnp.minimum(target - first * LEAVES_DEV, leaves)] += tile_apply(
                source_aug[unit], target_aug[unit], buf[slot, unit, D:ROWS]
            )

    for leaf in range(leaves):
        start = leaf % LEAVES_DEV * LEAF
        out_ref[leaf // LEAVES_DEV, :, start : start + LEAF] = acc[leaf].astype(out_ref.dtype)


def near_part(pairs, count, targets, sources, first, devices, seed, dtype, expected):
    seeds = [] if seed is None else [seed]
    return pl.pallas_call(
        functools.partial(near_kernel, first, devices, len(sources), seed is not None),
        out_shape=jax.ShapeDtypeStruct((devices, RHS, P_DEV), dtype),
        in_specs=[SMEM, SMEM, ANY] + [ANY] * len(sources) + [VMEM] * len(seeds),
        out_specs=VMEM,
        scratch_shapes=[
            pltpu.VMEM((2, UNROLL, ROWS, LEAF), jnp.bfloat16),
            pltpu.VMEM((2, UNROLL, D, LEAF), jnp.bfloat16),
            pltpu.SemaphoreType.DMA((2, UNROLL, 2)),
            pltpu.VMEM((UNROLL, DEPTH, LEAF), jnp.bfloat16),
            pltpu.VMEM((UNROLL, DEPTH, LEAF), jnp.bfloat16),
            pltpu.VMEM((devices * LEAVES_DEV + 1, RHS, LEAF), jnp.float32),
        ],
        compiler_params=pltpu.CompilerParams(vmem_limit_bytes=32 << 20),
        cost_estimate=cost(expected * LEAF * LEAF, 8 << 20),
    )(pairs, count, targets, *sources, *seeds)


def fold(weights):
    half = weights.shape[-1] // 2
    summed = weights[:, :half].astype(jnp.float32) + weights[:, half:].astype(jnp.float32)
    return summed.astype(jnp.bfloat16)


def fold_node(node):
    half = SKEL // 2
    return jnp.concatenate([node[:D, :half], fold(node[D:])], axis=0)


def sibling_nodes(base, place):
    found = []
    current = base
    steps = [("core", 1)] + [(axis, bit) for axis in ("y", "x", "z") for bit in (1, 2)]
    for level, (axis, bit) in enumerate(steps):
        partner = swap(current, axis, bit)
        found.append(partner)
        if level + 1 < len(steps):
            upper = (place[axis] // bit) % 2
            mine, theirs = fold_node(current), fold_node(partner)
            current = jnp.concatenate(
                [jnp.where(upper == 0, mine, theirs), jnp.where(upper == 0, theirs, mine)], axis=1
            )
    return jnp.stack(found)


def pair_lists(near_leaf, near_count, place):
    rows, counts = [], []
    for core in (1 - place["core"], place["core"]):
        for by in LINE:
            y = (place["y"] + by) % SIZES["y"]
            device = ((place["z"] * 4 + place["x"]) * 4 + y) * 2 + core
            rows.append(lax.dynamic_slice_in_dim(near_leaf, device * LEAVES_DEV, LEAVES_DEV))
            counts.append(lax.dynamic_slice_in_dim(near_count, device * LEAVES_DEV, LEAVES_DEV))
    leaf_ids = jnp.concatenate(rows, axis=0).reshape(-1)
    used = jnp.arange(NEAR, dtype=jnp.int32)[None, :] < jnp.concatenate(counts, axis=0)[:, None]
    used = used.reshape(-1)
    owner, local = leaf_ids // LEAVES_DEV, leaf_ids % LEAVES_DEV
    valid = used & (owner // 2 % 4 == place["y"]) & (local // CLASS == place["core"])
    back_z, back_x = (place["z"] - owner // 32) % 4, (place["x"] - owner // 8) % 4
    on_z = place["core"] == 0
    inner, outer = jnp.where(on_z, back_z, back_x), jnp.where(on_z, back_x, back_z)
    inner, outer = (jnp.where(back == 0, 0, jnp.where(back == 1, 1, 5 - back)) for back in (inner, outer))
    which = outer * 2 + (owner % 2 != place["core"]).astype(jnp.int32)
    late = which >= 6
    at = jnp.arange(leaf_ids.shape[0], dtype=jnp.int32)
    target = at // NEAR
    code = ((target * 8 + jnp.where(late, which - 6, which)) * 4 + inner) * CLASS + local % CLASS
    group = jnp.where(target < 32, 1, jnp.where(target < 56, 2, 3))
    group = jnp.where(valid, jnp.where(late, group, 0), -1)
    rank = jnp.sum(((group[None, :] == group[:, None]) & (at[None, :] < at[:, None])).astype(jnp.int32), axis=1)
    base = jnp.zeros_like(group)
    for index, start in enumerate(STARTS):
        base = jnp.where(group == index, start, base)
    goal = jnp.where(valid, base + rank, -1)
    place_at = jnp.arange(sum(LISTS), dtype=jnp.int32)
    hit = goal[None, :] == place_at[:, None]
    packed = jnp.sum(jnp.where(hit, code[None, :] + 1, 0), axis=1)
    packed = jnp.where(packed == 0, SPARE * 32 * CLASS, packed - 1)
    totals = jnp.sum((group[None, :] == jnp.arange(len(LISTS), dtype=jnp.int32)[:, None]).astype(jnp.int32), axis=1)
    return (
        [packed[s : s + n] for s, n in zip(STARTS, LISTS)],
        [totals[i : i + 1] for i in range(len(LISTS))],
    )


def spread(own, other, stage):
    ahead, ahead_other = ring(own, 1, stage), ring(other, 1, stage)
    behind_other, behind = ring(other, -1, stage), ring(own, -1, stage)
    across, across_other = ring(ahead, 1, stage), ring(behind_other, -1, stage)
    return (own, ahead, behind, across), (other, ahead_other, behind_other, across_other)


def per_device(points, weights, skel_index, assign, near_leaf, near_count):
    place = {axis: lax.axis_index(axis) for axis in AXES}
    core = place["core"]
    width = CLASS * LEAF

    def leaf_class(which):
        return jnp.concatenate(
            [lax.dynamic_slice_in_dim(a, which * width, width, axis=1) for a in (points, weights)], axis=0
        )

    own, other = spread(leaf_class(core), swap(leaf_class(1 - core), "core", 1), 0)
    own, other = spread(jnp.stack(own), jnp.stack(other), 1)

    line = jnp.stack([shift(points, "y", -by) if by else points for by in LINE])
    targets = jnp.concatenate([swap(line, "core", 1), line], axis=0)

    member = (assign[None, :] == jnp.arange(SKEL, dtype=jnp.int32)[:, None]).astype(jnp.bfloat16)
    base_weights = lax.dot_general(
        weights, member, (((1,), (1,)), ((), ())), preferred_element_type=jnp.float32
    )
    base = jnp.concatenate([points[:, skel_index], base_weights.astype(jnp.bfloat16)], axis=0)
    nodes = sibling_nodes(base, place)
    self_sum = self_terms(points, weights)
    far_field = far_terms(points, nodes)

    pairs, totals = pair_lists(near_leaf, near_count, place)
    early = [own[0], other[0], own[1], other[1], own[2], other[2]]
    late = [own[3], other[3]]
    early_sum = near_part(pairs[0], totals[0], targets, early, 0, 8, None, jnp.float32, 72)
    early_sum, late = lax.optimization_barrier((early_sum, late))
    across = near_part(pairs[1], totals[1], targets, late, 0, 4, early_sum[0:4], jnp.bfloat16, 12)
    across = swap(across, "core", 1)
    along = near_part(pairs[2], totals[2], targets, late, 4, 3, early_sum[4:7], jnp.float32, 9)
    home = near_part(pairs[3], totals[3], targets, late, 7, 1, early_sum[7:8], jnp.float32, 3)
    near_sum = self_sum + home[0] + across[3].astype(jnp.float32)
    for at, by in enumerate(LINE[:3]):
        part = (along[at] + across[at].astype(jnp.float32)).astype(jnp.bfloat16)
        near_sum = near_sum + shift(part, "y", by).astype(jnp.float32)
    return (near_sum * NEAR_SCALE, far_field)


def solution(mesh):
    grid = Mesh(mesh.devices.reshape([SIZES[axis] for axis in AXES]), AXES)
    split = P(None, AXES)
    return jax.shard_map(
        per_device,
        mesh=grid,
        in_specs=(split, split, P(AXES), P(AXES), P(), P()),
        out_specs=(split, split),
        check_vma=False,
    )
```

```python
import functools
import math

import jax
import jax.numpy as jnp
from jax import lax
from jax.experimental import pallas as pl
from jax.experimental.pallas import tpu as pltpu
from jax.sharding import Mesh, PartitionSpec as P

D = 64
RHS = 32
LEAF = 512
SKEL = 512
NEAR = 12
LEAVES_DEV = 8
P_DEV = LEAF * LEAVES_DEV
ROWS = D + RHS
N_DEV = 128
LEVELS = 7
SIZES = {"z": 4, "x": 4, "y": 4, "core": 2}
AXES = ("z", "x", "y", "core")
DEPTH = D + 16
UNROLL = 4
GAIN = 2.0 * math.log2(math.e) / D
NEAR_SCALE = 4.0 / math.sqrt(LEAF * (NEAR + 1))
FAR_SCALE = 4.0 / math.sqrt(P_DEV * N_DEV)
LINE = (2, 1, 3, 0)
CLASS = LEAVES_DEV // 2
LISTS = (64, 128, 32, 32)
STARTS = (0, 64, 192, 224)
SPARE = 2 * len(LINE) * LEAVES_DEV


def shift(block, axis, by):
    count = SIZES[axis]
    return lax.ppermute(block, axis, [(i, (i + by) % count) for i in range(count)])


def swap(block, axis, bit):
    count = SIZES[axis]
    return lax.ppermute(block, axis, [(i, i ^ bit) for i in range(count)])


def ring(block, by, stage):
    route = []
    for flat in range(N_DEV):
        z, x, y, core = flat // 32, flat // 8 % 4, flat // 2 % 4, flat % 2
        if core == stage:
            z = (z + by) % 4
        else:
            x = (x + by) % 4
        route.append((flat, ((z * 4 + x) * 4 + y) * 2 + core))
    return lax.ppermute(block, AXES, route)


def put_points(aug, coords, first):
    width = coords.shape[1]
    aug[0:D, :] = coords
    wide = coords.astype(jnp.float32)
    rest = jnp.sum(wide * wide, axis=0, keepdims=True) * -0.5
    row = lax.broadcasted_iota(jnp.int32, (16, width), 0)
    rows = jnp.where(row < 6, 1.0, 0.0)
    for part in range(3):
        piece = rest.astype(jnp.bfloat16).astype(jnp.float32)
        rest = rest - piece
        rows = jnp.where(row == first + part, piece, rows)
    aug[D:, :] = rows.astype(jnp.bfloat16)


def tile_apply(source_aug, target_aug, source_w):
    power = lax.dot_general(
        source_aug, target_aug, (((0,), (0,)), ((), ())), preferred_element_type=jnp.float32
    )
    tile = jnp.exp2(power * GAIN).astype(jnp.bfloat16)
    return jnp.dot(source_w, tile, preferred_element_type=jnp.float32)


def cost(entries, moved):
    return pl.CostEstimate(
        flops=int(entries) * 2 * (DEPTH + RHS), transcendentals=int(entries), bytes_accessed=moved
    )


VMEM = pl.BlockSpec(memory_space=pltpu.VMEM)
SMEM = pl.BlockSpec(memory_space=pltpu.SMEM)
ANY = pl.BlockSpec(memory_space=pl.ANY)


def self_kernel(points_ref, weights_ref, out_ref, target_aug, source_aug):
    @pl.loop(0, LEAVES_DEV // UNROLL)
    def _(group):
        for unit in range(UNROLL):
            start = pl.multiple_of((group * UNROLL + unit) * LEAF, LEAF)
            cols = pl.ds(start, LEAF)
            put_points(source_aug.at[unit], points_ref[:, cols], 0)
            put_points(target_aug.at[unit], points_ref[:, cols], 3)
            out_ref[:, cols] = tile_apply(source_aug[unit], target_aug[unit], weights_ref[:, cols])


def self_terms(points, weights):
    return pl.pallas_call(
        self_kernel,
        out_shape=jax.ShapeDtypeStruct((RHS, P_DEV), jnp.float32),
        in_specs=[VMEM, VMEM],
        out_specs=VMEM,
        scratch_shapes=[pltpu.VMEM((UNROLL, DEPTH, LEAF), jnp.bfloat16)] * 2,
        compiler_params=pltpu.CompilerParams(vmem_limit_bytes=24 << 20),
        cost_estimate=cost(LEAF * P_DEV, 2 << 20),
    )(points, weights)


def far_kernel(me_ref, points_ref, partner_ref, skel_ref, far_ref, coords, heavy, folded, sem, target_aug, source_aug):
    me = me_ref[0]
    half = SKEL // 2
    copies = [pltpu.make_async_copy(skel_ref.at[:, D:ROWS, :], folded, sem.at[0])]
    spans = []
    for level in range(1, LEVELS):
        low = ((me >> level) ^ 1) << level
        for side in range(2):
            start = low + side * (1 << (level - 1))
            cols = slice(side * half, (side + 1) * half)
            spans.append((level, cols, start))
            copies.append(
                pltpu.make_async_copy(
                    skel_ref.at[start, 0:D, :], coords.at[level, :, cols], sem.at[len(copies)]
                )
            )
    for copy in copies:
        copy.start()
    for leaf in range(LEAVES_DEV):
        cols = slice(leaf * LEAF, (leaf + 1) * LEAF)
        put_points(target_aug.at[:, cols], points_ref[:, cols], 3)
    coords[0] = partner_ref[0:D, :]
    heavy[0] = partner_ref[D:ROWS, :]
    far_ref[...] = jnp.zeros_like(far_ref)
    for copy in copies:
        copy.wait()
    for level, cols, start in spans:

        def add(at, total, start=start):
            return total + folded[start + at].astype(jnp.float32)

        total = lax.fori_loop(0, 1 << (level - 1), add, jnp.zeros((RHS, half), jnp.float32))
        heavy[level, :, cols] = total.astype(jnp.bfloat16)

    @pl.loop(0, LEVELS)
    def _(level):
        put_points(source_aug, coords[level], 0)
        far_ref[...] += tile_apply(source_aug[...], target_aug[...], heavy[level])

    far_ref[...] = far_ref[...] * FAR_SCALE


def far_terms(me, points, partner, skeletons):
    half = SKEL // 2
    return pl.pallas_call(
        far_kernel,
        out_shape=jax.ShapeDtypeStruct((RHS, P_DEV), jnp.float32),
        in_specs=[SMEM, VMEM, VMEM, ANY],
        out_specs=VMEM,
        scratch_shapes=[
            pltpu.VMEM((LEVELS, D, SKEL), jnp.bfloat16),
            pltpu.VMEM((LEVELS, RHS, SKEL), jnp.bfloat16),
            pltpu.VMEM((N_DEV, RHS, half), jnp.bfloat16),
            pltpu.SemaphoreType.DMA((2 * LEVELS - 1,)),
            pltpu.VMEM((DEPTH, P_DEV), jnp.bfloat16),
            pltpu.VMEM((DEPTH, SKEL), jnp.bfloat16),
        ],
        compiler_params=pltpu.CompilerParams(vmem_limit_bytes=24 << 20),
        cost_estimate=cost(LEVELS * SKEL * P_DEV, 4 << 20),
    )(me, points, partner, skeletons)


def near_kernel(first, devices, n_source, seeded, pair_ref, count_ref, target_ref, *refs):
    source_refs, refs = refs[:n_source], refs[n_source:]
    if seeded:
        seed_ref, refs = refs[0], refs[1:]
    out_ref, buf, target_buf, sem, target_aug, source_aug, acc = refs
    leaves = devices * LEAVES_DEV
    groups = (count_ref[0] + (UNROLL - 1)) // UNROLL

    def fetch(group, slot):
        for unit in range(UNROLL):
            code = pair_ref[group * UNROLL + unit]
            target = code // (256 * CLASS)
            start = pl.multiple_of(target % LEAVES_DEV * LEAF, LEAF)
            pltpu.make_async_copy(
                target_ref.at[code // (32 * CLASS) % 8, :, pl.ds(start, LEAF)],
                target_buf.at[slot, unit],
                sem.at[slot, unit, 1],
            ).start()
            which = code // (4 * CLASS) % 8
            start = pl.multiple_of(code % CLASS * LEAF, LEAF)
            for at in range(n_source):

                @pl.when(which == at)
                def _():
                    pltpu.make_async_copy(
                        source_refs[at].at[code // CLASS % 4, :, pl.ds(start, LEAF)],
                        buf.at[slot, unit],
                        sem.at[slot, unit, 0],
                    ).start()

    def arrive(slot):
        for unit in range(UNROLL):
            pltpu.make_async_copy(
                source_refs[0].at[0, :, pl.ds(0, LEAF)], buf.at[slot, unit], sem.at[slot, unit, 0]
            ).wait()
            pltpu.make_async_copy(
                target_ref.at[0, :, pl.ds(0, LEAF)], target_buf.at[slot, unit], sem.at[slot, unit, 1]
            ).wait()

    @pl.when(groups > 0)
    def _():
        fetch(0, 0)

    if seeded:
        for leaf in range(leaves):
            start = leaf % LEAVES_DEV * LEAF
            acc[leaf] = seed_ref[leaf // LEAVES_DEV, :, start : start + LEAF]
    else:
        acc[...] = jnp.zeros_like(acc)

    @pl.loop(0, groups)
    def _(group):
        slot = group % 2

        @pl.when(group + 1 < groups)
        def _():
            fetch(group + 1, 1 - slot)

        arrive(slot)
        for unit in range(UNROLL):
            target = pair_ref[group * UNROLL + unit] // (256 * CLASS)
            put_points(source_aug.at[unit], buf[slot, unit, 0:D], 0)
            put_points(target_aug.at[unit], target_buf[slot, unit], 3)
            acc[jnp.minimum(target - first * LEAVES_DEV, leaves)] += tile_apply(
                source_aug[unit], target_aug[unit], buf[slot, unit, D:ROWS]
            )

    for leaf in range(leaves):
        start = leaf % LEAVES_DEV * LEAF
        out_ref[leaf // LEAVES_DEV, :, start : start + LEAF] = acc[leaf].astype(out_ref.dtype)


def near_part(pairs, count, targets, sources, first, devices, seed, dtype, expected):
    seeds = [] if seed is None else [seed]
    return pl.pallas_call(
        functools.partial(near_kernel, first, devices, len(sources), seed is not None),
        out_shape=jax.ShapeDtypeStruct((devices, RHS, P_DEV), dtype),
        in_specs=[SMEM, SMEM, ANY] + [ANY] * len(sources) + [VMEM] * len(seeds),
        out_specs=VMEM,
        scratch_shapes=[
            pltpu.VMEM((2, UNROLL, ROWS, LEAF), jnp.bfloat16),
            pltpu.VMEM((2, UNROLL, D, LEAF), jnp.bfloat16),
            pltpu.SemaphoreType.DMA((2, UNROLL, 2)),
            pltpu.VMEM((UNROLL, DEPTH, LEAF), jnp.bfloat16),
            pltpu.VMEM((UNROLL, DEPTH, LEAF), jnp.bfloat16),
            pltpu.VMEM((devices * LEAVES_DEV + 1, RHS, LEAF), jnp.float32),
        ],
        compiler_params=pltpu.CompilerParams(vmem_limit_bytes=32 << 20),
        cost_estimate=cost(expected * LEAF * LEAF, 8 << 20),
    )(pairs, count, targets, *sources, *seeds)


def fold(weights):
    half = weights.shape[-1] // 2
    summed = weights[:, :half].astype(jnp.float32) + weights[:, half:].astype(jnp.float32)
    return summed.astype(jnp.bfloat16)


def pair_lists(near_leaf, near_count, place):
    rows, counts, lines = [], [], []
    for core in (1 - place["core"], place["core"]):
        for by in LINE:
            y = (place["y"] + by) % SIZES["y"]
            device = ((place["z"] * 4 + place["x"]) * 4 + y) * 2 + core
            lines.append(y * 2 + core)
            rows.append(lax.dynamic_slice_in_dim(near_leaf, device * LEAVES_DEV, LEAVES_DEV))
            counts.append(lax.dynamic_slice_in_dim(near_count, device * LEAVES_DEV, LEAVES_DEV))
    leaf_ids = jnp.concatenate(rows, axis=0).reshape(-1)
    used = jnp.arange(NEAR, dtype=jnp.int32)[None, :] < jnp.concatenate(counts, axis=0)[:, None]
    used = used.reshape(-1)
    owner, local = leaf_ids // LEAVES_DEV, leaf_ids % LEAVES_DEV
    valid = used & (owner // 2 % 4 == place["y"]) & (local // CLASS == place["core"])
    back_z, back_x = (place["z"] - owner // 32) % 4, (place["x"] - owner // 8) % 4
    on_z = place["core"] == 0
    inner, outer = jnp.where(on_z, back_z, back_x), jnp.where(on_z, back_x, back_z)
    inner, outer = (jnp.where(back == 0, 0, jnp.where(back == 1, 1, 5 - back)) for back in (inner, outer))
    other = (owner % 2 != place["core"]).astype(jnp.int32)
    at = jnp.arange(leaf_ids.shape[0], dtype=jnp.int32)
    target = at // NEAR
    line = jnp.repeat(jnp.stack(lines), LEAVES_DEV * NEAR, total_repeat_length=leaf_ids.shape[0])
    which = jnp.where((outer == 1) | (outer == 2), outer - 1 + 2 * other, other)
    code = (((target * 8 + line) * 8 + which) * 4 + inner) * CLASS + local % CLASS
    group = jnp.where(outer == 0, 0, jnp.where(outer < 3, 1, jnp.where(target < SPARE // 2, 2, 3)))
    group = jnp.where(valid, group, -1)
    rank = jnp.sum(((group[None, :] == group[:, None]) & (at[None, :] < at[:, None])).astype(jnp.int32), axis=1)
    base = jnp.zeros_like(group)
    for index, start in enumerate(STARTS):
        base = jnp.where(group == index, start, base)
    goal = jnp.where(valid, base + rank, -1)
    place_at = jnp.arange(sum(LISTS), dtype=jnp.int32)
    hit = goal[None, :] == place_at[:, None]
    packed = jnp.sum(jnp.where(hit, code[None, :] + 1, 0), axis=1)
    packed = jnp.where(packed == 0, SPARE * 256 * CLASS, packed - 1)
    totals = jnp.sum((group[None, :] == jnp.arange(len(LISTS), dtype=jnp.int32)[:, None]).astype(jnp.int32), axis=1)
    return (
        [packed[s : s + n] for s, n in zip(STARTS, LISTS)],
        [totals[i : i + 1] for i in range(len(LISTS))],
    )


def spread(own, other, stage):
    ahead, behind_other = ring(own, 1, stage), ring(other, -1, stage)
    ahead_other, behind = ring(other, 1, stage), ring(own, -1, stage)
    return (ahead, behind), (ahead_other, behind_other)


def spread_on(own, other, stage):
    return ring(own[0], 1, stage), ring(other[1], -1, stage)


def per_device(points, weights, skel_index, assign, near_leaf, near_count):
    place = {axis: lax.axis_index(axis) for axis in AXES}
    core = place["core"]
    width = CLASS * LEAF

    def leaf_class(which):
        return jnp.concatenate(
            [lax.dynamic_slice_in_dim(a, which * width, width, axis=1) for a in (points, weights)], axis=0
        )

    targets = lax.all_gather(points, ("y", "core"))
    mine, theirs = leaf_class(core), leaf_class(1 - core)
    theirs = swap(theirs, "core", 1)
    own, other = spread(mine, theirs, 0)
    own_far, other_far = spread_on(own, other, 0)
    _, assign, skel_index = lax.optimization_barrier((own[0], assign, skel_index))
    own_line = jnp.stack([mine, *own, own_far])
    other_line = jnp.stack([theirs, *other, other_far])
    own, other = spread(own_line, other_line, 1)

    member = (assign[None, :] == jnp.arange(SKEL, dtype=jnp.int32)[:, None]).astype(jnp.bfloat16)
    base_weights = lax.dot_general(
        weights, member, (((1,), (1,)), ((), ())), preferred_element_type=jnp.float32
    ).astype(jnp.bfloat16)
    base = jnp.concatenate([points[:, skel_index], base_weights], axis=0)
    folded = jnp.concatenate([base[:D, : SKEL // 2], fold(base_weights)], axis=0)
    skeletons = lax.all_gather(folded, AXES)
    me = ((place["z"] * 4 + place["x"]) * 4 + place["y"]) * 2 + core
    far_field = far_terms(me.reshape(1), points, swap(base, "core", 1), skeletons)
    self_sum = self_terms(points, weights)

    pairs, totals = pair_lists(near_leaf, near_count, place)
    seed = near_part(pairs[0], totals[0], targets, [own_line, other_line], 0, 8, None, jnp.float32, 24)
    seed, own, other = lax.optimization_barrier((seed, own, other))
    late = spread_on(own, other, 1)
    seed = near_part(pairs[1], totals[1], targets, [*own, *other], 0, 8, seed, jnp.float32, 48)
    across = near_part(pairs[2], totals[2], targets, late, 0, 4, seed[0:4], jnp.bfloat16, 12)
    across = swap(across, "core", 1)
    along = near_part(pairs[3], totals[3], targets, late, 4, 4, seed[4:8], jnp.float32, 12)
    parts = [
        shift((along[at] + across[at].astype(jnp.float32)).astype(jnp.bfloat16), "y", by)
        for at, by in enumerate(LINE[:3])
    ]
    near_sum = self_sum + along[3] + across[3].astype(jnp.float32)
    near_sum, parts, far_field = lax.optimization_barrier((near_sum, parts, far_field))
    for part in parts:
        near_sum = near_sum + part.astype(jnp.float32)
    return (near_sum * NEAR_SCALE, far_field)


def solution(mesh):
    grid = Mesh(mesh.devices.reshape([SIZES[axis] for axis in AXES]), AXES)
    split = P(None, AXES)
    return jax.shard_map(
        per_device,
        mesh=grid,
        in_specs=(split, split, P(AXES), P(AXES), P(), P()),
        out_specs=(split, split),
        check_vma=False,
    )
```

```python
import functools
import math

import jax
import jax.numpy as jnp
from jax import lax
from jax.experimental import pallas as pl
from jax.experimental.pallas import tpu as pltpu
from jax.sharding import Mesh, PartitionSpec as P

D = 64
RHS = 32
LEAF = 512
SKEL = 512
NEAR = 12
LEAVES_DEV = 8
P_DEV = LEAF * LEAVES_DEV
ROWS = D + RHS
N_DEV = 128
SIZES = {"z": 4, "x": 4, "y": 4, "core": 2}
AXES = ("z", "x", "y", "core")
DEPTH = D + 16
UNROLL = 4
GAIN = 2.0 * math.log2(math.e) / D
NEAR_SCALE = 4.0 / math.sqrt(LEAF * (NEAR + 1))
FAR_SCALE = 4.0 / math.sqrt(P_DEV * N_DEV)
CLASS = LEAVES_DEV // 2
LISTS = (96, 128, 32)
STARTS = (0, 96, 224)
SPARE = 8 * LEAVES_DEV


def shift(block, axis, by):
    count = SIZES[axis]
    return lax.ppermute(block, axis, [(i, (i + by) % count) for i in range(count)])


def swap(block, axis, bit):
    count = SIZES[axis]
    return lax.ppermute(block, axis, [(i, i ^ bit) for i in range(count)])


def ring(block, by, stage):
    route = []
    for flat in range(N_DEV):
        z, x, y, core = flat // 32, flat // 8 % 4, flat // 2 % 4, flat % 2
        if core == stage:
            z = (z + by) % 4
        else:
            x = (x + by) % 4
        route.append((flat, ((z * 4 + x) * 4 + y) * 2 + core))
    return lax.ppermute(block, AXES, route)


def put_points(aug, coords, first):
    width = coords.shape[1]
    aug[0:D, :] = coords
    wide = coords.astype(jnp.float32)
    rest = jnp.sum(wide * wide, axis=0, keepdims=True) * -0.5
    row = lax.broadcasted_iota(jnp.int32, (16, width), 0)
    rows = jnp.where(row < 6, 1.0, 0.0)
    for part in range(3):
        piece = rest.astype(jnp.bfloat16).astype(jnp.float32)
        rest = rest - piece
        rows = jnp.where(row == first + part, piece, rows)
    aug[D:, :] = rows.astype(jnp.bfloat16)


def tile_apply(source_aug, target_aug, source_w):
    power = lax.dot_general(
        source_aug, target_aug, (((0,), (0,)), ((), ())), preferred_element_type=jnp.float32
    )
    tile = jnp.exp2(power * GAIN).astype(jnp.bfloat16)
    return jnp.dot(source_w, tile, preferred_element_type=jnp.float32)


def cost(entries, moved):
    return pl.CostEstimate(
        flops=int(entries) * 16 * (DEPTH + RHS), transcendentals=int(entries), bytes_accessed=moved
    )


VMEM = pl.BlockSpec(memory_space=pltpu.VMEM)
SMEM = pl.BlockSpec(memory_space=pltpu.SMEM)
ANY = pl.BlockSpec(memory_space=pl.ANY)


def self_kernel(points_ref, weights_ref, out_ref, target_aug, source_aug):
    @pl.loop(0, LEAVES_DEV // UNROLL)
    def _(group):
        for unit in range(UNROLL):
            start = pl.multiple_of((group * UNROLL + unit) * LEAF, LEAF)
            cols = pl.ds(start, LEAF)
            put_points(source_aug.at[unit], points_ref[:, cols], 0)
            put_points(target_aug.at[unit], points_ref[:, cols], 3)
            out_ref[:, cols] = tile_apply(source_aug[unit], target_aug[unit], weights_ref[:, cols])


def self_terms(points, weights):
    return pl.pallas_call(
        self_kernel,
        out_shape=jax.ShapeDtypeStruct((RHS, P_DEV), jnp.float32),
        in_specs=[VMEM, VMEM],
        out_specs=VMEM,
        scratch_shapes=[pltpu.VMEM((UNROLL, DEPTH, LEAF), jnp.bfloat16)] * 2,
        compiler_params=pltpu.CompilerParams(vmem_limit_bytes=24 << 20),
        cost_estimate=cost(LEAF * P_DEV, 2 << 20),
    )(points, weights)


def put_node(ref, coords_ref, heavy_ref, start, depth):
    half = SKEL // 2
    for side in range(2):
        cols = slice(side * half, (side + 1) * half)
        lead = start + side * (1 << (depth - 1))
        coords_ref[:, cols] = ref[lead, 0:D, 0:half]
        total = jnp.zeros((RHS, half), jnp.float32)
        for at in range(1 << (depth - 1)):
            heavy = ref[lead + at, D:ROWS].astype(jnp.float32)
            total = total + (heavy if ref.shape[-1] == half else heavy[:, :half] + heavy[:, half:])
        heavy_ref[:, cols] = total.astype(jnp.bfloat16)


def merge_kernel(nodes_ref, node_ref, out_ref):
    half = SKEL // 2
    put_node(nodes_ref, node_ref.at[0:D], node_ref.at[D:ROWS], 0, 3)
    heavy = node_ref[D:ROWS].astype(jnp.float32)
    out_ref[0, 0:D] = node_ref[0:D, 0:half]
    out_ref[0, D:ROWS] = (heavy[:, :half] + heavy[:, half:]).astype(jnp.bfloat16)
    for copy in range(1, 16):
        out_ref[copy] = out_ref[0]


def merge(nodes):
    return pl.pallas_call(
        merge_kernel,
        out_shape=(
            jax.ShapeDtypeStruct((ROWS, SKEL), jnp.bfloat16),
            jax.ShapeDtypeStruct((16, ROWS, SKEL // 2), jnp.bfloat16),
        ),
        in_specs=[VMEM],
        out_specs=(VMEM, VMEM),
        compiler_params=pltpu.CompilerParams(vmem_limit_bytes=8 << 20),
        cost_estimate=cost(0, 1 << 20),
    )(nodes)


def far_kernel(depths, seeded, place_ref, points_ref, sibling_ref, nodes_ref, *refs):
    if seeded:
        seed_ref, refs = refs[0], refs[1:]
    far_ref, coords, heavy, target_aug, source_aug = refs
    for leaf in range(LEAVES_DEV):
        cols = slice(leaf * LEAF, (leaf + 1) * LEAF)
        put_points(target_aug.at[:, cols], points_ref[:, cols], 3)
    coords[0] = sibling_ref[0:D]
    heavy[0] = sibling_ref[D:ROWS]
    for depth in range(1, depths):
        start = ((place_ref[0] >> depth) ^ 1) << depth
        put_node(nodes_ref, coords.at[depth], heavy.at[depth], start, depth)
    far_ref[...] = seed_ref[...] if seeded else jnp.zeros_like(far_ref)

    @pl.loop(0, depths)
    def _(at):
        put_points(source_aug, coords[at], 0)
        far_ref[...] += tile_apply(source_aug[...], target_aug[...], heavy[at])

    if seeded:
        far_ref[...] = far_ref[...] * FAR_SCALE


def far_terms(place, points, sibling, nodes, depths, seed=None):
    seeds = [] if seed is None else [seed]
    return pl.pallas_call(
        functools.partial(far_kernel, depths, seed is not None),
        out_shape=jax.ShapeDtypeStruct((RHS, P_DEV), jnp.float32),
        in_specs=[SMEM, VMEM, VMEM, VMEM] + [VMEM] * len(seeds),
        out_specs=VMEM,
        scratch_shapes=[
            pltpu.VMEM((depths, D, SKEL), jnp.bfloat16),
            pltpu.VMEM((depths, RHS, SKEL), jnp.bfloat16),
            pltpu.VMEM((DEPTH, P_DEV), jnp.bfloat16),
            pltpu.VMEM((DEPTH, SKEL), jnp.bfloat16),
        ],
        compiler_params=pltpu.CompilerParams(vmem_limit_bytes=24 << 20),
        cost_estimate=cost(depths * SKEL * P_DEV, 4 << 20),
    )(place.reshape(1), points, sibling, nodes, *seeds)


def near_kernel(first, devices, n_source, seeded, pair_ref, count_ref, other_ref, line_ref, *refs):
    source_refs, refs = refs[:n_source], refs[n_source:]
    if seeded:
        seed_ref, refs = refs[0], refs[1:]
    out_ref, buf, target_buf, sem, whole_sem, target_aug, source_aug, acc = refs
    groups = (count_ref[0] + (UNROLL - 1)) // UNROLL

    def fetch(group, slot):
        for unit in range(UNROLL):
            code = pair_ref[group * UNROLL + unit]
            target = jnp.minimum(code // (32 * CLASS), SPARE - 1)
            start = pl.multiple_of(target % LEAVES_DEV * LEAF, LEAF)
            device = target // LEAVES_DEV
            for ref, here in ((other_ref, device < 4), (line_ref, device >= 4)):

                @pl.when(here)
                def _(ref=ref):
                    pltpu.make_async_copy(
                        ref.at[device % 4, :, pl.ds(start, LEAF)],
                        target_buf.at[slot, unit],
                        sem.at[slot, unit, 1],
                    ).start()

            which = code // (4 * CLASS) % 8
            start = pl.multiple_of(code % CLASS * LEAF, LEAF)
            for at in range(n_source):

                @pl.when(which == at)
                def _():
                    pltpu.make_async_copy(
                        source_refs[at].at[code // CLASS % 4, :, pl.ds(start, LEAF)],
                        buf.at[slot, unit],
                        sem.at[slot, unit, 0],
                    ).start()

    def arrive(slot):
        for unit in range(UNROLL):
            pltpu.make_async_copy(
                source_refs[0].at[0, :, pl.ds(0, LEAF)], buf.at[slot, unit], sem.at[slot, unit, 0]
            ).wait()
            pltpu.make_async_copy(
                line_ref.at[0, :, pl.ds(0, LEAF)], target_buf.at[slot, unit], sem.at[slot, unit, 1]
            ).wait()

    @pl.when(groups > 0)
    def _():
        fetch(0, 0)

    total = acc.at[pl.ds(0, devices)]
    if seeded:
        seed = pltpu.make_async_copy(seed_ref, total, whole_sem)
        seed.start()
        seed.wait()
    else:
        acc[...] = jnp.zeros_like(acc)

    @pl.loop(0, groups)
    def _(group):
        slot = group % 2

        @pl.when(group + 1 < groups)
        def _():
            fetch(group + 1, 1 - slot)

        arrive(slot)
        for unit in range(UNROLL):
            target = pair_ref[group * UNROLL + unit] // (32 * CLASS)
            put_points(source_aug.at[unit], buf[slot, unit, 0:D], 0)
            put_points(target_aug.at[unit], target_buf[slot, unit], 3)
            start = pl.multiple_of(target % LEAVES_DEV * LEAF, LEAF)
            acc[jnp.minimum(target // LEAVES_DEV - first, devices), :, pl.ds(start, LEAF)] += tile_apply(
                source_aug[unit], target_aug[unit], buf[slot, unit, D:ROWS]
            )

    if out_ref.dtype == jnp.float32:
        result = pltpu.make_async_copy(total, out_ref, whole_sem)
        result.start()
        result.wait()
    else:
        out_ref[...] = total[...].astype(out_ref.dtype)


def near_part(pairs, count, targets, sources, first, devices, seed, dtype, expected):
    seeds = [] if seed is None else [seed]
    return pl.pallas_call(
        functools.partial(near_kernel, first, devices, len(sources), seed is not None),
        out_shape=jax.ShapeDtypeStruct((devices, RHS, P_DEV), dtype),
        in_specs=[SMEM, SMEM, ANY, ANY] + [ANY] * len(sources) + [ANY] * len(seeds),
        out_specs=ANY if dtype == jnp.float32 else VMEM,
        scratch_shapes=[
            pltpu.VMEM((2, UNROLL, ROWS, LEAF), jnp.bfloat16),
            pltpu.VMEM((2, UNROLL, D, LEAF), jnp.bfloat16),
            pltpu.SemaphoreType.DMA((2, UNROLL, 2)),
            pltpu.SemaphoreType.DMA,
            pltpu.VMEM((UNROLL, DEPTH, LEAF), jnp.bfloat16),
            pltpu.VMEM((UNROLL, DEPTH, LEAF), jnp.bfloat16),
            pltpu.VMEM((devices + 1, RHS, P_DEV), jnp.float32),
        ],
        compiler_params=pltpu.CompilerParams(vmem_limit_bytes=32 << 20),
        cost_estimate=cost(expected * LEAF * LEAF, 8 << 20),
    )(pairs, count, *targets, *sources, *seeds)


def exchange(copies, axis):
    return lax.all_to_all(copies, axis, split_axis=0, concat_axis=0, tiled=True)


def everyone(block, axes):
    count = math.prod(SIZES[axis] for axis in axes)
    return exchange(jnp.broadcast_to(block[None], (count, *block.shape)), axes)


def pair_lists(near_leaf, near_count, place):
    rows, counts = [], []
    for core in (1 - place["core"], place["core"]):
        for y in range(SIZES["y"]):
            device = ((place["z"] * 4 + place["x"]) * 4 + y) * 2 + core
            rows.append(lax.dynamic_slice_in_dim(near_leaf, device * LEAVES_DEV, LEAVES_DEV))
            counts.append(lax.dynamic_slice_in_dim(near_count, device * LEAVES_DEV, LEAVES_DEV))
    leaf_ids = jnp.concatenate(rows, axis=0).reshape(-1)
    used = jnp.arange(NEAR, dtype=jnp.int32)[None, :] < jnp.concatenate(counts, axis=0)[:, None]
    used = used.reshape(-1)
    owner, local = leaf_ids // LEAVES_DEV, leaf_ids % LEAVES_DEV
    valid = used & (owner // 2 % 4 == place["y"]) & (local // CLASS == place["core"])
    back_z, back_x = (place["z"] - owner // 32) % 4, (place["x"] - owner // 8) % 4
    on_z = place["core"] == 0
    inner, outer = jnp.where(on_z, back_z, back_x), jnp.where(on_z, back_x, back_z)
    inner, outer = (jnp.where(back == 0, 0, jnp.where(back == 1, 1, 5 - back)) for back in (inner, outer))
    other = (owner % 2 != place["core"]).astype(jnp.int32)
    at = jnp.arange(leaf_ids.shape[0], dtype=jnp.int32)
    target = at // NEAR
    first = target < SPARE // 2
    which = outer * 2 + other - jnp.where((outer == 3) & ~first, 6, 0)
    code = ((target * 8 + which) * 4 + inner) * CLASS + local % CLASS
    group = jnp.where(first, 1, jnp.where(outer == 3, 2, 0))
    group = jnp.where(valid, group, -1)
    rank = jnp.sum(((group[None, :] == group[:, None]) & (at[None, :] < at[:, None])).astype(jnp.int32), axis=1)
    base = jnp.zeros_like(group)
    for index, start in enumerate(STARTS):
        base = jnp.where(group == index, start, base)
    goal = jnp.where(valid, base + rank, -1)
    place_at = jnp.arange(sum(LISTS), dtype=jnp.int32)
    hit = goal[None, :] == place_at[:, None]
    packed = jnp.sum(jnp.where(hit, code[None, :] + 1, 0), axis=1)
    packed = jnp.where(packed == 0, SPARE * 32 * CLASS, packed - 1)
    totals = jnp.sum((group[None, :] == jnp.arange(len(LISTS), dtype=jnp.int32)[:, None]).astype(jnp.int32), axis=1)
    return (
        [packed[s : s + n] for s, n in zip(STARTS, LISTS)],
        [totals[i : i + 1] for i in range(len(LISTS))],
    )


def spread(own, other, stage):
    ahead, behind_other = ring(own, 1, stage), ring(other, -1, stage)
    ahead_other, behind = ring(other, 1, stage), ring(own, -1, stage)
    return (ahead, behind), (ahead_other, behind_other)


def spread_on(own, other, stage):
    return ring(own[0], 1, stage), ring(other[1], -1, stage)


def leaf_class(points, weights, which):
    width = CLASS * LEAF
    return jnp.concatenate(
        [lax.dynamic_slice_in_dim(a, which * width, width, axis=1) for a in (points, weights)], axis=0
    )


def per_device(points, weights, skel_index, assign, near_leaf, near_count):
    place = {axis: lax.axis_index(axis) for axis in AXES}
    core = place["core"]
    mine = leaf_class(points, weights, core)
    theirs = swap(leaf_class(points, weights, 1 - core), "core", 1)
    own, other = spread(mine, theirs, 0)
    _, _, points_later = lax.optimization_barrier((own, other, points))
    own_far, other_far = spread_on(own, other, 0)
    line = everyone(points_later, ("y",))
    own_far, other_far = lax.optimization_barrier((own_far, other_far))
    own_line = jnp.stack([mine, *own, own_far])
    other_line = jnp.stack([theirs, *other, other_far])
    own, other = spread(own_line, other_line, 1)

    _, _, assign, skel_index = lax.optimization_barrier((own_line, other_line, assign, skel_index))
    member = (assign[None, :] == jnp.arange(SKEL, dtype=jnp.int32)[:, None]).astype(jnp.bfloat16)
    base_weights = lax.dot_general(
        weights, member, (((1,), (1,)), ((), ())), preferred_element_type=jnp.float32
    ).astype(jnp.bfloat16)
    base = jnp.concatenate([points[:, skel_index], base_weights], axis=0)
    near_nodes = everyone(base, ("y", "core"))
    targets = (swap(line, "core", 1), line)
    node, copies = merge(near_nodes)
    in_line = place["y"] * 2 + core
    core_sibling = lax.dynamic_index_in_dim(near_nodes, in_line ^ 1, 0, keepdims=False)

    pairs, totals = pair_lists(near_leaf, near_count, place)
    early = [own_line, other_line, own[0], other[0], own[1], other[1]]
    late = spread_on(own, other, 1)
    home = near_part(pairs[0], totals[0], (line, line), early, 4, 4, None, jnp.float32, 36)
    cross_pairs, home, copies, node = lax.optimization_barrier((pairs[1], home, copies, node))
    x_sibling = swap(node, "x", 1)
    wide_nodes = exchange(copies, ("z", "x"))
    across = near_part(cross_pairs, totals[1], targets, [*early, *late], 0, 4, None, jnp.bfloat16, 48)
    last_pairs, across, x_sibling, wide_nodes = lax.optimization_barrier((pairs[2], across, x_sibling, wide_nodes))
    across = swap(across, "core", 1)
    home = near_part(last_pairs, totals[2], (line, line), late, 4, 4, home, jnp.float32, 12)
    parts = exchange((home + across.astype(jnp.float32)).astype(jnp.bfloat16), "y")
    _, points_later = lax.optimization_barrier((home, points))
    self_sum = self_terms(points_later, weights)
    far_field = far_terms(in_line, points, core_sibling, near_nodes, 3)
    far_field = far_terms(place["z"] * 4 + place["x"], points, x_sibling, wide_nodes, 4, far_field)
    parts, far_field, self_sum = lax.optimization_barrier((parts, far_field, self_sum))
    near_sum = self_sum + jnp.sum(parts.astype(jnp.float32), axis=0)
    return (near_sum * NEAR_SCALE, far_field)


def solution(mesh):
    grid = Mesh(mesh.devices.reshape([SIZES[axis] for axis in AXES]), AXES)
    split = P(None, AXES)
    return jax.shard_map(
        per_device,
        mesh=grid,
        in_specs=(split, split, P(AXES), P(AXES), P(), P()),
        out_specs=(split, split),
        check_vma=False,
    )
```

```python
import functools
import math

import jax
import jax.numpy as jnp
from jax import lax
from jax.experimental import pallas as pl
from jax.experimental.pallas import tpu as pltpu
from jax.sharding import Mesh, PartitionSpec as P

D = 64
RHS = 32
LEAF = 512
SKEL = 512
NEAR = 12
LEAVES_DEV = 8
P_DEV = LEAF * LEAVES_DEV
ROWS = D + RHS
N_DEV = 128
SIZES = {"z": 4, "x": 4, "y": 4, "core": 2}
AXES = ("z", "x", "y", "core")
DEPTH = D + 16
UNROLL = 4
GAIN = 2.0 * math.log2(math.e) / D
NEAR_SCALE = 4.0 / math.sqrt(LEAF * (NEAR + 1))
FAR_SCALE = 4.0 / math.sqrt(P_DEV * N_DEV)
CLASS = LEAVES_DEV // 2
LISTS = (96, 128, 32)
STARTS = (0, 96, 224)
SPARE = 8 * LEAVES_DEV


def shift(block, axis, by):
    count = SIZES[axis]
    return lax.ppermute(block, axis, [(i, (i + by) % count) for i in range(count)])


def swap(block, axis, bit):
    count = SIZES[axis]
    return lax.ppermute(block, axis, [(i, i ^ bit) for i in range(count)])


def ring(block, by, stage):
    route = []
    for flat in range(N_DEV):
        z, x, y, core = flat // 32, flat // 8 % 4, flat // 2 % 4, flat % 2
        if core == stage:
            z = (z + by) % 4
        else:
            x = (x + by) % 4
        route.append((flat, ((z * 4 + x) * 4 + y) * 2 + core))
    return lax.ppermute(block, AXES, route)


def put_points(aug, coords, first):
    width = coords.shape[1]
    aug[0:D, :] = coords
    wide = coords.astype(jnp.float32)
    rest = jnp.sum(wide * wide, axis=0, keepdims=True) * -0.5
    row = lax.broadcasted_iota(jnp.int32, (16, width), 0)
    rows = jnp.where(row < 6, 1.0, 0.0)
    for part in range(3):
        piece = rest.astype(jnp.bfloat16).astype(jnp.float32)
        rest = rest - piece
        rows = jnp.where(row == first + part, piece, rows)
    aug[D:, :] = rows.astype(jnp.bfloat16)


def tile_apply(source_aug, target_aug, source_w):
    power = lax.dot_general(
        source_aug, target_aug, (((0,), (0,)), ((), ())), preferred_element_type=jnp.float32
    )
    tile = jnp.exp2(power * GAIN).astype(jnp.bfloat16)
    return jnp.dot(source_w, tile, preferred_element_type=jnp.float32)


def cost(entries, moved):
    return pl.CostEstimate(
        flops=int(entries) * 16 * (DEPTH + RHS), transcendentals=int(entries), bytes_accessed=moved
    )


VMEM = pl.BlockSpec(memory_space=pltpu.VMEM)
SMEM = pl.BlockSpec(memory_space=pltpu.SMEM)
ANY = pl.BlockSpec(memory_space=pl.ANY)


def self_kernel(points_ref, weights_ref, out_ref, target_aug, source_aug):
    @pl.loop(0, LEAVES_DEV // UNROLL)
    def _(group):
        for unit in range(UNROLL):
            start = pl.multiple_of((group * UNROLL + unit) * LEAF, LEAF)
            cols = pl.ds(start, LEAF)
            put_points(source_aug.at[unit], points_ref[:, cols], 0)
            put_points(target_aug.at[unit], points_ref[:, cols], 3)
            out_ref[:, cols] = tile_apply(source_aug[unit], target_aug[unit], weights_ref[:, cols])


def self_terms(points, weights):
    return pl.pallas_call(
        self_kernel,
        out_shape=jax.ShapeDtypeStruct((RHS, P_DEV), jnp.float32),
        in_specs=[VMEM, VMEM],
        out_specs=VMEM,
        scratch_shapes=[pltpu.VMEM((UNROLL, DEPTH, LEAF), jnp.bfloat16)] * 2,
        compiler_params=pltpu.CompilerParams(vmem_limit_bytes=24 << 20),
        cost_estimate=cost(LEAF * P_DEV, 2 << 20),
    )(points, weights)


def put_node(ref, coords_ref, heavy_ref, start, depth):
    half = SKEL // 2
    for side in range(2):
        cols = slice(side * half, (side + 1) * half)
        lead = start + side * (1 << (depth - 1))
        coords_ref[:, cols] = ref[lead, 0:D, 0:half]
        total = jnp.zeros((RHS, half), jnp.float32)
        for at in range(1 << (depth - 1)):
            heavy = ref[lead + at, D:ROWS].astype(jnp.float32)
            total = total + (heavy if ref.shape[-1] == half else heavy[:, :half] + heavy[:, half:])
        heavy_ref[:, cols] = total.astype(jnp.bfloat16)


def merge_kernel(nodes_ref, node_ref, out_ref):
    half = SKEL // 2
    put_node(nodes_ref, node_ref.at[0:D], node_ref.at[D:ROWS], 0, 3)
    heavy = node_ref[D:ROWS].astype(jnp.float32)
    out_ref[0, 0:D] = node_ref[0:D, 0:half]
    out_ref[0, D:ROWS] = (heavy[:, :half] + heavy[:, half:]).astype(jnp.bfloat16)
    for copy in range(1, 16):
        out_ref[copy] = out_ref[0]


def merge(nodes):
    return pl.pallas_call(
        merge_kernel,
        out_shape=(
            jax.ShapeDtypeStruct((ROWS, SKEL), jnp.bfloat16),
            jax.ShapeDtypeStruct((16, ROWS, SKEL // 2), jnp.bfloat16),
        ),
        in_specs=[VMEM],
        out_specs=(VMEM, VMEM),
        compiler_params=pltpu.CompilerParams(vmem_limit_bytes=8 << 20),
        cost_estimate=cost(0, 1 << 20),
    )(nodes)


def far_kernel(depths, seeded, place_ref, points_ref, sibling_ref, nodes_ref, *refs):
    if seeded:
        seed_ref, refs = refs[0], refs[1:]
    far_ref, coords, heavy, target_aug, source_aug = refs
    for leaf in range(LEAVES_DEV):
        cols = slice(leaf * LEAF, (leaf + 1) * LEAF)
        put_points(target_aug.at[:, cols], points_ref[:, cols], 3)
    coords[0] = sibling_ref[0:D]
    heavy[0] = sibling_ref[D:ROWS]
    for depth in range(1, depths):
        start = ((place_ref[0] >> depth) ^ 1) << depth
        put_node(nodes_ref, coords.at[depth], heavy.at[depth], start, depth)
    far_ref[...] = seed_ref[...] if seeded else jnp.zeros_like(far_ref)

    @pl.loop(0, depths)
    def _(at):
        put_points(source_aug, coords[at], 0)
        far_ref[...] += tile_apply(source_aug[...], target_aug[...], heavy[at])

    if seeded:
        far_ref[...] = far_ref[...] * FAR_SCALE


def far_terms(place, points, sibling, nodes, depths, seed=None):
    seeds = [] if seed is None else [seed]
    return pl.pallas_call(
        functools.partial(far_kernel, depths, seed is not None),
        out_shape=jax.ShapeDtypeStruct((RHS, P_DEV), jnp.float32),
        in_specs=[SMEM, VMEM, VMEM, VMEM] + [VMEM] * len(seeds),
        out_specs=VMEM,
        scratch_shapes=[
            pltpu.VMEM((depths, D, SKEL), jnp.bfloat16),
            pltpu.VMEM((depths, RHS, SKEL), jnp.bfloat16),
            pltpu.VMEM((DEPTH, P_DEV), jnp.bfloat16),
            pltpu.VMEM((DEPTH, SKEL), jnp.bfloat16),
        ],
        compiler_params=pltpu.CompilerParams(vmem_limit_bytes=24 << 20),
        cost_estimate=cost(depths * SKEL * P_DEV, 4 << 20),
    )(place.reshape(1), points, sibling, nodes, *seeds)


def near_kernel(first, devices, n_source, seeded, pair_ref, count_ref, other_ref, line_ref, *refs):
    source_refs, refs = refs[:n_source], refs[n_source:]
    if seeded:
        seed_ref, refs = refs[0], refs[1:]
    out_ref, buf, target_buf, sem, whole_sem, target_aug, source_aug, acc = refs
    groups = (count_ref[0] + (UNROLL - 1)) // UNROLL

    def fetch(group, slot):
        for unit in range(UNROLL):
            code = pair_ref[group * UNROLL + unit]
            target = jnp.minimum(code // (32 * CLASS), SPARE - 1)
            start = pl.multiple_of(target % LEAVES_DEV * LEAF, LEAF)
            device = target // LEAVES_DEV
            for ref, here in ((other_ref, device < 4), (line_ref, device >= 4)):

                @pl.when(here)
                def _(ref=ref):
                    pltpu.make_async_copy(
                        ref.at[device % 4, :, pl.ds(start, LEAF)],
                        target_buf.at[slot, unit],
                        sem.at[slot, unit, 1],
                    ).start()

            which = code // (4 * CLASS) % 8
            start = pl.multiple_of(code % CLASS * LEAF, LEAF)
            for at in range(n_source):

                @pl.when(which == at)
                def _():
                    pltpu.make_async_copy(
                        source_refs[at].at[code // CLASS % 4, :, pl.ds(start, LEAF)],
                        buf.at[slot, unit],
                        sem.at[slot, unit, 0],
                    ).start()

    def arrive(slot):
        for unit in range(UNROLL):
            pltpu.make_async_copy(
                source_refs[0].at[0, :, pl.ds(0, LEAF)], buf.at[slot, unit], sem.at[slot, unit, 0]
            ).wait()
            pltpu.make_async_copy(
                line_ref.at[0, :, pl.ds(0, LEAF)], target_buf.at[slot, unit], sem.at[slot, unit, 1]
            ).wait()

    @pl.when(groups > 0)
    def _():
        fetch(0, 0)

    total = acc.at[pl.ds(0, devices)]
    if seeded:
        seed = pltpu.make_async_copy(seed_ref, total, whole_sem)
        seed.start()
        seed.wait()
    else:
        acc[...] = jnp.zeros_like(acc)

    @pl.loop(0, groups)
    def _(group):
        slot = group % 2

        @pl.when(group + 1 < groups)
        def _():
            fetch(group + 1, 1 - slot)

        arrive(slot)
        for unit in range(UNROLL):
            target = pair_ref[group * UNROLL + unit] // (32 * CLASS)
            put_points(source_aug.at[unit], buf[slot, unit, 0:D], 0)
            put_points(target_aug.at[unit], target_buf[slot, unit], 3)
            start = pl.multiple_of(target % LEAVES_DEV * LEAF, LEAF)
            acc[jnp.minimum(target // LEAVES_DEV - first, devices), :, pl.ds(start, LEAF)] += tile_apply(
                source_aug[unit], target_aug[unit], buf[slot, unit, D:ROWS]
            )

    if out_ref.dtype == jnp.float32:
        result = pltpu.make_async_copy(total, out_ref, whole_sem)
        result.start()
        result.wait()
    else:
        out_ref[...] = total[...].astype(out_ref.dtype)


def near_part(pairs, count, targets, sources, first, devices, seed, dtype, expected):
    seeds = [] if seed is None else [seed]
    return pl.pallas_call(
        functools.partial(near_kernel, first, devices, len(sources), seed is not None),
        out_shape=jax.ShapeDtypeStruct((devices, RHS, P_DEV), dtype),
        in_specs=[SMEM, SMEM, ANY, ANY] + [ANY] * len(sources) + [ANY] * len(seeds),
        out_specs=ANY if dtype == jnp.float32 else VMEM,
        scratch_shapes=[
            pltpu.VMEM((2, UNROLL, ROWS, LEAF), jnp.bfloat16),
            pltpu.VMEM((2, UNROLL, D, LEAF), jnp.bfloat16),
            pltpu.SemaphoreType.DMA((2, UNROLL, 2)),
            pltpu.SemaphoreType.DMA,
            pltpu.VMEM((UNROLL, DEPTH, LEAF), jnp.bfloat16),
            pltpu.VMEM((UNROLL, DEPTH, LEAF), jnp.bfloat16),
            pltpu.VMEM((devices + 1, RHS, P_DEV), jnp.float32),
        ],
        compiler_params=pltpu.CompilerParams(vmem_limit_bytes=32 << 20),
        cost_estimate=cost(expected * LEAF * LEAF, 8 << 20),
    )(pairs, count, *targets, *sources, *seeds)


def exchange(copies, axis):
    return lax.all_to_all(copies, axis, split_axis=0, concat_axis=0, tiled=True)


def everyone(block, axes):
    count = math.prod(SIZES[axis] for axis in axes)
    return exchange(jnp.broadcast_to(block[None], (count, *block.shape)), axes)


def pair_lists(near_leaf, near_count, place):
    rows, counts = [], []
    for core in (1 - place["core"], place["core"]):
        for y in range(SIZES["y"]):
            device = ((place["z"] * 4 + place["x"]) * 4 + y) * 2 + core
            rows.append(lax.dynamic_slice_in_dim(near_leaf, device * LEAVES_DEV, LEAVES_DEV))
            counts.append(lax.dynamic_slice_in_dim(near_count, device * LEAVES_DEV, LEAVES_DEV))
    leaf_ids = jnp.concatenate(rows, axis=0).reshape(-1)
    used = jnp.arange(NEAR, dtype=jnp.int32)[None, :] < jnp.concatenate(counts, axis=0)[:, None]
    used = used.reshape(-1)
    owner, local = leaf_ids // LEAVES_DEV, leaf_ids % LEAVES_DEV
    valid = used & (owner // 2 % 4 == place["y"]) & (local // CLASS == place["core"])
    back_z, back_x = (place["z"] - owner // 32) % 4, (place["x"] - owner // 8) % 4
    on_z = place["core"] == 0
    inner, outer = jnp.where(on_z, back_z, back_x), jnp.where(on_z, back_x, back_z)
    inner, outer = (jnp.where(back == 0, 0, jnp.where(back == 1, 1, 5 - back)) for back in (inner, outer))
    other = (owner % 2 != place["core"]).astype(jnp.int32)
    at = jnp.arange(leaf_ids.shape[0], dtype=jnp.int32)
    target = at // NEAR
    first = target < SPARE // 2
    which = outer * 2 + other - jnp.where((outer == 3) & ~first, 6, 0)
    code = ((target * 8 + which) * 4 + inner) * CLASS + local % CLASS
    group = jnp.where(first, 1, jnp.where(outer == 3, 2, 0))
    group = jnp.where(valid, group, -1)
    rank = jnp.sum(((group[None, :] == group[:, None]) & (at[None, :] < at[:, None])).astype(jnp.int32), axis=1)
    base = jnp.zeros_like(group)
    for index, start in enumerate(STARTS):
        base = jnp.where(group == index, start, base)
    goal = jnp.where(valid, base + rank, -1)
    place_at = jnp.arange(sum(LISTS), dtype=jnp.int32)
    hit = goal[None, :] == place_at[:, None]
    packed = jnp.sum(jnp.where(hit, code[None, :] + 1, 0), axis=1)
    packed = jnp.where(packed == 0, SPARE * 32 * CLASS, packed - 1)
    totals = jnp.sum((group[None, :] == jnp.arange(len(LISTS), dtype=jnp.int32)[:, None]).astype(jnp.int32), axis=1)
    return (
        [packed[s : s + n] for s, n in zip(STARTS, LISTS)],
        [totals[i : i + 1] for i in range(len(LISTS))],
    )


def spread(own, other, stage):
    ahead, behind_other = ring(own, 1, stage), ring(other, -1, stage)
    ahead_other, behind = ring(other, 1, stage), ring(own, -1, stage)
    return (ahead, behind), (ahead_other, behind_other)


def spread_on(own, other, stage):
    return ring(own[0], 1, stage), ring(other[1], -1, stage)


def leaf_class(points, weights, which):
    width = CLASS * LEAF
    return jnp.concatenate(
        [lax.dynamic_slice_in_dim(a, which * width, width, axis=1) for a in (points, weights)], axis=0
    )


def per_device(points, weights, skel_index, assign, near_leaf, near_count):
    place = {axis: lax.axis_index(axis) for axis in AXES}
    core = place["core"]
    mine = leaf_class(points, weights, core)
    theirs = swap(leaf_class(points, weights, 1 - core), "core", 1)
    own, other = spread(mine, theirs, 0)
    own_far, other_far = spread_on(own, other, 0)
    line = everyone(points, ("y",))
    own_far, other_far = lax.optimization_barrier((own_far, other_far))
    own_line = jnp.stack([mine, *own, own_far])
    other_line = jnp.stack([theirs, *other, other_far])
    own, other = spread(own_line, other_line, 1)

    _, _, assign, skel_index = lax.optimization_barrier((own_line, other_line, assign, skel_index))
    member = (assign[None, :] == jnp.arange(SKEL, dtype=jnp.int32)[:, None]).astype(jnp.bfloat16)
    base_weights = lax.dot_general(
        weights, member, (((1,), (1,)), ((), ())), preferred_element_type=jnp.float32
    ).astype(jnp.bfloat16)
    base = jnp.concatenate([points[:, skel_index], base_weights], axis=0)
    near_nodes = everyone(base, ("y", "core"))
    targets = (swap(line, "core", 1), line)
    node, copies = merge(near_nodes)
    in_line = place["y"] * 2 + core
    core_sibling = lax.dynamic_index_in_dim(near_nodes, in_line ^ 1, 0, keepdims=False)

    pairs, totals = pair_lists(near_leaf, near_count, place)
    early = [own_line, other_line, own[0], other[0], own[1], other[1]]
    late = spread_on(own, other, 1)
    self_sum = self_terms(points, weights)
    home_pairs, self_sum = lax.optimization_barrier((pairs[0], self_sum))
    home = near_part(home_pairs, totals[0], (line, line), early, 4, 4, None, jnp.float32, 36)
    cross_pairs, home, copies, node = lax.optimization_barrier((pairs[1], home, copies, node))
    x_sibling = swap(node, "x", 1)
    wide_nodes = exchange(copies, ("z", "x"))
    across = near_part(cross_pairs, totals[1], targets, [*early, *late], 0, 4, None, jnp.bfloat16, 48)
    last_pairs, across, x_sibling, wide_nodes = lax.optimization_barrier((pairs[2], across, x_sibling, wide_nodes))
    across = swap(across, "core", 1)
    home = near_part(last_pairs, totals[2], (line, line), late, 4, 4, home, jnp.float32, 12)
    parts = (home + across.astype(jnp.float32)).astype(jnp.bfloat16)
    parts, points_last = lax.optimization_barrier((parts, points))
    parts = exchange(parts, "y")
    _, points_later = lax.optimization_barrier((home, points))
    far_field = far_terms(in_line, points_last, core_sibling, near_nodes, 3)
    far_field = far_terms(place["z"] * 4 + place["x"], points, x_sibling, wide_nodes, 4, far_field)
    parts, far_field, self_sum = lax.optimization_barrier((parts, far_field, self_sum))
    near_sum = self_sum + jnp.sum(parts.astype(jnp.float32), axis=0)
    return (near_sum * NEAR_SCALE, far_field)


def solution(mesh):
    grid = Mesh(mesh.devices.reshape([SIZES[axis] for axis in AXES]), AXES)
    split = P(None, AXES)
    return jax.shard_map(
        per_device,
        mesh=grid,
        in_specs=(split, split, P(AXES), P(AXES), P(), P()),
        out_specs=(split, split),
        check_vma=False,
    )
```

```python
import functools
import math

import jax
import jax.numpy as jnp
from jax import lax
from jax.experimental import pallas as pl
from jax.experimental.pallas import tpu as pltpu
from jax.sharding import Mesh, PartitionSpec as P

D = 64
RHS = 32
LEAF = 512
SKEL = 512
NEAR = 12
LEAVES_DEV = 8
P_DEV = LEAF * LEAVES_DEV
ROWS = D + RHS
N_DEV = 128
SIZES = {"z": 4, "x": 4, "y": 4, "core": 2}
AXES = ("z", "x", "y", "core")
DEPTH = D + 16
UNROLL = 4
GAIN = 2.0 * math.log2(math.e) / D
NEAR_SCALE = 4.0 / math.sqrt(LEAF * (NEAR + 1))
FAR_SCALE = 4.0 / math.sqrt(P_DEV * N_DEV)
CLASS = LEAVES_DEV // 2
LISTS = (96, 128, 32)
STARTS = (0, 96, 224)
SPARE = 8 * LEAVES_DEV


def shift(block, axis, by):
    count = SIZES[axis]
    return lax.ppermute(block, axis, [(i, (i + by) % count) for i in range(count)])


def swap(block, axis, bit):
    count = SIZES[axis]
    return lax.ppermute(block, axis, [(i, i ^ bit) for i in range(count)])


def ring(block, by, stage):
    route = []
    for flat in range(N_DEV):
        z, x, y, core = flat // 32, flat // 8 % 4, flat // 2 % 4, flat % 2
        if core == stage:
            z = (z + by) % 4
        else:
            x = (x + by) % 4
        route.append((flat, ((z * 4 + x) * 4 + y) * 2 + core))
    return lax.ppermute(block, AXES, route)


def put_points(aug, coords, first):
    width = coords.shape[1]
    aug[0:D, :] = coords
    wide = coords.astype(jnp.float32)
    rest = jnp.sum(wide * wide, axis=0, keepdims=True) * -0.5
    row = lax.broadcasted_iota(jnp.int32, (16, width), 0)
    rows = jnp.where(row < 6, 1.0, 0.0)
    for part in range(3):
        piece = rest.astype(jnp.bfloat16).astype(jnp.float32)
        rest = rest - piece
        rows = jnp.where(row == first + part, piece, rows)
    aug[D:, :] = rows.astype(jnp.bfloat16)


def tile_apply(source_aug, target_aug, source_w):
    power = lax.dot_general(
        source_aug, target_aug, (((0,), (0,)), ((), ())), preferred_element_type=jnp.float32
    )
    tile = jnp.exp2(power * GAIN).astype(jnp.bfloat16)
    return jnp.dot(source_w, tile, preferred_element_type=jnp.float32)


def cost(entries, moved):
    return pl.CostEstimate(
        flops=int(entries) * 16 * (DEPTH + RHS), transcendentals=int(entries), bytes_accessed=moved
    )


VMEM = pl.BlockSpec(memory_space=pltpu.VMEM)
SMEM = pl.BlockSpec(memory_space=pltpu.SMEM)
ANY = pl.BlockSpec(memory_space=pl.ANY)


def self_kernel(points_ref, weights_ref, out_ref, target_aug, source_aug):
    @pl.loop(0, LEAVES_DEV // UNROLL)
    def _(group):
        for unit in range(UNROLL):
            start = pl.multiple_of((group * UNROLL + unit) * LEAF, LEAF)
            cols = pl.ds(start, LEAF)
            put_points(source_aug.at[unit], points_ref[:, cols], 0)
            put_points(target_aug.at[unit], points_ref[:, cols], 3)
            out_ref[:, cols] = tile_apply(source_aug[unit], target_aug[unit], weights_ref[:, cols])


def self_terms(points, weights):
    return pl.pallas_call(
        self_kernel,
        out_shape=jax.ShapeDtypeStruct((RHS, P_DEV), jnp.float32),
        in_specs=[VMEM, VMEM],
        out_specs=VMEM,
        scratch_shapes=[pltpu.VMEM((UNROLL, DEPTH, LEAF), jnp.bfloat16)] * 2,
        compiler_params=pltpu.CompilerParams(vmem_limit_bytes=24 << 20),
        cost_estimate=cost(LEAF * P_DEV, 2 << 20),
    )(points, weights)


def put_node(ref, coords_ref, heavy_ref, start, depth):
    half = SKEL // 2
    for side in range(2):
        cols = slice(side * half, (side + 1) * half)
        lead = start + side * (1 << (depth - 1))
        coords_ref[:, cols] = ref[lead, 0:D, 0:half]
        total = jnp.zeros((RHS, half), jnp.float32)
        for at in range(1 << (depth - 1)):
            heavy = ref[lead + at, D:ROWS].astype(jnp.float32)
            total = total + (heavy if ref.shape[-1] == half else heavy[:, :half] + heavy[:, half:])
        heavy_ref[:, cols] = total.astype(jnp.bfloat16)


def merge_kernel(nodes_ref, node_ref, out_ref):
    half = SKEL // 2
    put_node(nodes_ref, node_ref.at[0:D], node_ref.at[D:ROWS], 0, 3)
    heavy = node_ref[D:ROWS].astype(jnp.float32)
    out_ref[0, 0:D] = node_ref[0:D, 0:half]
    out_ref[0, D:ROWS] = (heavy[:, :half] + heavy[:, half:]).astype(jnp.bfloat16)
    for copy in range(1, 16):
        out_ref[copy] = out_ref[0]


def merge(nodes):
    return pl.pallas_call(
        merge_kernel,
        out_shape=(
            jax.ShapeDtypeStruct((ROWS, SKEL), jnp.bfloat16),
            jax.ShapeDtypeStruct((16, ROWS, SKEL // 2), jnp.bfloat16),
        ),
        in_specs=[VMEM],
        out_specs=(VMEM, VMEM),
        compiler_params=pltpu.CompilerParams(vmem_limit_bytes=8 << 20),
        cost_estimate=cost(0, 1 << 20),
    )(nodes)


def far_kernel(depths, seeded, place_ref, points_ref, sibling_ref, nodes_ref, *refs):
    if seeded:
        seed_ref, refs = refs[0], refs[1:]
    far_ref, coords, heavy, target_aug, source_aug = refs
    for leaf in range(LEAVES_DEV):
        cols = slice(leaf * LEAF, (leaf + 1) * LEAF)
        put_points(target_aug.at[:, cols], points_ref[:, cols], 3)
    coords[0] = sibling_ref[0:D]
    heavy[0] = sibling_ref[D:ROWS]
    for depth in range(1, depths):
        start = ((place_ref[0] >> depth) ^ 1) << depth
        put_node(nodes_ref, coords.at[depth], heavy.at[depth], start, depth)
    far_ref[...] = seed_ref[...] if seeded else jnp.zeros_like(far_ref)

    @pl.loop(0, depths)
    def _(at):
        put_points(source_aug, coords[at], 0)
        far_ref[...] += tile_apply(source_aug[...], target_aug[...], heavy[at])

    if seeded:
        far_ref[...] = far_ref[...] * FAR_SCALE


def far_terms(place, points, sibling, nodes, depths, seed=None):
    seeds = [] if seed is None else [seed]
    return pl.pallas_call(
        functools.partial(far_kernel, depths, seed is not None),
        out_shape=jax.ShapeDtypeStruct((RHS, P_DEV), jnp.float32),
        in_specs=[SMEM, VMEM, VMEM, VMEM] + [VMEM] * len(seeds),
        out_specs=VMEM,
        scratch_shapes=[
            pltpu.VMEM((depths, D, SKEL), jnp.bfloat16),
            pltpu.VMEM((depths, RHS, SKEL), jnp.bfloat16),
            pltpu.VMEM((DEPTH, P_DEV), jnp.bfloat16),
            pltpu.VMEM((DEPTH, SKEL), jnp.bfloat16),
        ],
        compiler_params=pltpu.CompilerParams(vmem_limit_bytes=24 << 20),
        cost_estimate=cost(depths * SKEL * P_DEV, 4 << 20),
    )(place.reshape(1), points, sibling, nodes, *seeds)


def near_kernel(first, devices, n_source, seeded, pair_ref, count_ref, target_ref, *refs):
    source_refs, refs = refs[:n_source], refs[n_source:]
    if seeded:
        seed_ref, refs = refs[0], refs[1:]
    out_ref, buf, target_buf, sem, whole_sem, target_aug, source_aug, acc = refs
    groups = (count_ref[0] + (UNROLL - 1)) // UNROLL

    def fetch(group, slot):
        for unit in range(UNROLL):
            code = pair_ref[group * UNROLL + unit]
            target = jnp.minimum(code // (32 * CLASS), SPARE - 1)
            start = pl.multiple_of(target % LEAVES_DEV * LEAF, LEAF)
            pltpu.make_async_copy(
                target_ref.at[target // LEAVES_DEV % 4, :, pl.ds(start, LEAF)],
                target_buf.at[slot, unit],
                sem.at[slot, unit, 1],
            ).start()
            which = code // (4 * CLASS) % 8
            start = pl.multiple_of(code % CLASS * LEAF, LEAF)
            for at in range(n_source):

                @pl.when(which == at)
                def _():
                    pltpu.make_async_copy(
                        source_refs[at].at[code // CLASS % 4, :, pl.ds(start, LEAF)],
                        buf.at[slot, unit],
                        sem.at[slot, unit, 0],
                    ).start()

    def arrive(slot):
        for unit in range(UNROLL):
            pltpu.make_async_copy(
                source_refs[0].at[0, :, pl.ds(0, LEAF)], buf.at[slot, unit], sem.at[slot, unit, 0]
            ).wait()
            pltpu.make_async_copy(
                target_ref.at[0, :, pl.ds(0, LEAF)], target_buf.at[slot, unit], sem.at[slot, unit, 1]
            ).wait()

    @pl.when(groups > 0)
    def _():
        fetch(0, 0)

    total = acc.at[pl.ds(0, devices)]
    if seeded:
        seed = pltpu.make_async_copy(seed_ref, total, whole_sem)
        seed.start()
        seed.wait()
    else:
        acc[...] = jnp.zeros_like(acc)

    @pl.loop(0, groups)
    def _(group):
        slot = group % 2

        @pl.when(group + 1 < groups)
        def _():
            fetch(group + 1, 1 - slot)

        arrive(slot)
        for unit in range(UNROLL):
            target = pair_ref[group * UNROLL + unit] // (32 * CLASS)
            put_points(source_aug.at[unit], buf[slot, unit, 0:D], 0)
            put_points(target_aug.at[unit], target_buf[slot, unit], 3)
            start = pl.multiple_of(target % LEAVES_DEV * LEAF, LEAF)
            acc[jnp.minimum(target // LEAVES_DEV - first, devices), :, pl.ds(start, LEAF)] += tile_apply(
                source_aug[unit], target_aug[unit], buf[slot, unit, D:ROWS]
            )

    if out_ref.dtype == jnp.float32:
        result = pltpu.make_async_copy(total, out_ref, whole_sem)
        result.start()
        result.wait()
    else:
        out_ref[...] = total[...].astype(out_ref.dtype)


def near_part(pairs, count, targets, sources, first, devices, seed, dtype, expected):
    seeds = [] if seed is None else [seed]
    return pl.pallas_call(
        functools.partial(near_kernel, first, devices, len(sources), seed is not None),
        out_shape=jax.ShapeDtypeStruct((devices, RHS, P_DEV), dtype),
        in_specs=[SMEM, SMEM, ANY] + [ANY] * len(sources) + [ANY] * len(seeds),
        out_specs=ANY if dtype == jnp.float32 else VMEM,
        scratch_shapes=[
            pltpu.VMEM((2, UNROLL, ROWS, LEAF), jnp.bfloat16),
            pltpu.VMEM((2, UNROLL, D, LEAF), jnp.bfloat16),
            pltpu.SemaphoreType.DMA((2, UNROLL, 2)),
            pltpu.SemaphoreType.DMA,
            pltpu.VMEM((UNROLL, DEPTH, LEAF), jnp.bfloat16),
            pltpu.VMEM((UNROLL, DEPTH, LEAF), jnp.bfloat16),
            pltpu.VMEM((devices + 1, RHS, P_DEV), jnp.float32),
        ],
        compiler_params=pltpu.CompilerParams(vmem_limit_bytes=18 << 20),
        cost_estimate=cost(expected * LEAF * LEAF, 8 << 20),
    )(pairs, count, targets, *sources, *seeds)


def exchange(copies, axis):
    return lax.all_to_all(copies, axis, split_axis=0, concat_axis=0, tiled=True)


def everyone(block, axes):
    count = math.prod(SIZES[axis] for axis in axes)
    return exchange(jnp.broadcast_to(block[None], (count, *block.shape)), axes)


def pair_lists(near_leaf, near_count, place):
    rows, counts = [], []
    for core in (1 - place["core"], place["core"]):
        for y in range(SIZES["y"]):
            device = ((place["z"] * 4 + place["x"]) * 4 + y) * 2 + core
            rows.append(lax.dynamic_slice_in_dim(near_leaf, device * LEAVES_DEV, LEAVES_DEV))
            counts.append(lax.dynamic_slice_in_dim(near_count, device * LEAVES_DEV, LEAVES_DEV))
    leaf_ids = jnp.concatenate(rows, axis=0).reshape(-1)
    used = jnp.arange(NEAR, dtype=jnp.int32)[None, :] < jnp.concatenate(counts, axis=0)[:, None]
    used = used.reshape(-1)
    owner, local = leaf_ids // LEAVES_DEV, leaf_ids % LEAVES_DEV
    valid = used & (owner // 2 % 4 == place["y"]) & (local // CLASS == place["core"])
    back_z, back_x = (place["z"] - owner // 32) % 4, (place["x"] - owner // 8) % 4
    on_z = place["core"] == 0
    inner, outer = jnp.where(on_z, back_z, back_x), jnp.where(on_z, back_x, back_z)
    inner, outer = (jnp.where(back == 0, 0, jnp.where(back == 1, 1, 5 - back)) for back in (inner, outer))
    other = (owner % 2 != place["core"]).astype(jnp.int32)
    at = jnp.arange(leaf_ids.shape[0], dtype=jnp.int32)
    target = at // NEAR
    first = target < SPARE // 2
    which = outer * 2 + other - jnp.where((outer == 3) & ~first, 6, 0)
    code = ((target * 8 + which) * 4 + inner) * CLASS + local % CLASS
    group = jnp.where(first, 1, jnp.where(outer == 3, 2, 0))
    group = jnp.where(valid, group, -1)
    rank = jnp.sum(((group[None, :] == group[:, None]) & (at[None, :] < at[:, None])).astype(jnp.int32), axis=1)
    base = jnp.zeros_like(group)
    for index, start in enumerate(STARTS):
        base = jnp.where(group == index, start, base)
    goal = jnp.where(valid, base + rank, -1)
    place_at = jnp.arange(sum(LISTS), dtype=jnp.int32)
    hit = goal[None, :] == place_at[:, None]
    packed = jnp.sum(jnp.where(hit, code[None, :] + 1, 0), axis=1)
    packed = jnp.where(packed == 0, SPARE * 32 * CLASS, packed - 1)
    totals = jnp.sum((group[None, :] == jnp.arange(len(LISTS), dtype=jnp.int32)[:, None]).astype(jnp.int32), axis=1)
    return (
        [packed[s : s + n] for s, n in zip(STARTS, LISTS)],
        [totals[i : i + 1] for i in range(len(LISTS))],
    )


def spread(own, other, stage):
    ahead, behind_other = ring(own, 1, stage), ring(other, -1, stage)
    ahead_other, behind = ring(other, 1, stage), ring(own, -1, stage)
    return (ahead, behind), (ahead_other, behind_other)


def spread_on(own, other, stage):
    return ring(own[0], 1, stage), ring(other[1], -1, stage)


def leaf_class(points, weights, which):
    width = CLASS * LEAF
    return jnp.concatenate(
        [lax.dynamic_slice_in_dim(a, which * width, width, axis=1) for a in (points, weights)], axis=0
    )


def per_device(points, weights, skel_index, assign, near_leaf, near_count):
    place = {axis: lax.axis_index(axis) for axis in AXES}
    core = place["core"]
    mine = leaf_class(points, weights, core)
    theirs = swap(leaf_class(points, weights, 1 - core), "core", 1)
    own, other = spread(mine, theirs, 0)
    own_far, other_far = spread_on(own, other, 0)
    line = everyone(points, ("y",))
    own_far, other_far = lax.optimization_barrier((own_far, other_far))
    own_line = jnp.stack([mine, *own, own_far])
    other_line = jnp.stack([theirs, *other, other_far])
    own, other = spread(own_line, other_line, 1)

    _, _, assign, skel_index = lax.optimization_barrier((own_line, other_line, assign, skel_index))
    member = (assign[None, :] == jnp.arange(SKEL, dtype=jnp.int32)[:, None]).astype(jnp.bfloat16)
    base_weights = lax.dot_general(
        weights, member, (((1,), (1,)), ((), ())), preferred_element_type=jnp.float32
    ).astype(jnp.bfloat16)
    base = jnp.concatenate([points[:, skel_index], base_weights], axis=0)
    near_nodes = everyone(base, ("y", "core"))
    other_targets = swap(line, "core", 1)
    node, copies = merge(near_nodes)
    in_line = place["y"] * 2 + core
    core_sibling = lax.dynamic_index_in_dim(near_nodes, in_line ^ 1, 0, keepdims=False)

    pairs, totals = pair_lists(near_leaf, near_count, place)
    early = [own_line, other_line, own[0], other[0], own[1], other[1]]
    late = spread_on(own, other, 1)
    self_sum = self_terms(points, weights)
    home_pairs, self_sum = lax.optimization_barrier((pairs[0], self_sum))
    home = near_part(home_pairs, totals[0], line, early, 4, 4, None, jnp.float32, 36)
    cross_pairs, home, copies, node = lax.optimization_barrier((pairs[1], home, copies, node))
    x_sibling = swap(node, "x", 1)
    wide_nodes = exchange(copies, ("z", "x"))
    across = near_part(cross_pairs, totals[1], other_targets, [*early, *late], 0, 4, None, jnp.bfloat16, 48)
    last_pairs, across, x_sibling, wide_nodes = lax.optimization_barrier((pairs[2], across, x_sibling, wide_nodes))
    across = swap(across, "core", 1)
    home = near_part(last_pairs, totals[2], line, late, 4, 4, home, jnp.float32, 12)
    parts = (home + across.astype(jnp.float32)).astype(jnp.bfloat16)
    parts, points_last = lax.optimization_barrier((parts, points))
    parts = exchange(parts, "y")
    far_field = far_terms(in_line, points_last, core_sibling, near_nodes, 3)
    far_field = far_terms(place["z"] * 4 + place["x"], points, x_sibling, wide_nodes, 4, far_field)
    parts, far_field, self_sum = lax.optimization_barrier((parts, far_field, self_sum))
    near_sum = self_sum
    for y in range(SIZES["y"]):
        near_sum = near_sum + parts[y].astype(jnp.float32)
    return (near_sum * NEAR_SCALE, far_field)


def solution(mesh):
    grid = Mesh(mesh.devices.reshape([SIZES[axis] for axis in AXES]), AXES)
    split = P(None, AXES)
    return jax.shard_map(
        per_device,
        mesh=grid,
        in_specs=(split, split, P(AXES), P(AXES), P(), P()),
        out_specs=(split, split),
        check_vma=False,
    )
```
